256 devices in a mesh: row: 8 (over x, core), col: 32 (over y, z).
Axes of the slice: x: 4, y: 4, z: 8, core: 2. Of those that a mesh axis runs over, the one named last changes fastest.
Arguments:
- upper_panel: float32 [2048, 8192], P('row', 'col')
- lower_panel: float32 [2048, 8192], P('row', 'col')
- pole_values: float32 [2, 8192], P(None, 'col'), may hold values from 0 to 4, as said below
- coupling: float32 [2, 8192], P(None, 'col'), may hold values from -6 to 6
- kept_mask: int32 [2, 8192], P(None, 'col'), may hold values from 0 to 1, as said below
- shifts: float32 [16384], P('col'), may hold values from 0 to 4
- source: int32 [16384], P('col'), may hold values from 0 to 16384, as said below
Outputs:
- vectors: float32 [2, 2048, 16384], P(None, 'row', 'col')
- slab_weight: float32 [16384], P('col')
The draws below stay inside these ranges and needn't reach their ends.
Inputs may be any that keep to these rules, and one draw needn't show every extreme that they name: source[j] = 16384 marks an undeflated merged column; any other value is the pole whose child column the merged column copies, and no pole is named twice. Each device's 512 merged columns hold from 64 to 384 undeflated columns, and some device holds exactly 384. kept_mask is 0 exactly at the poles named in source. Some device of col holds no deflated pole: every pole of both children that it holds is kept. `pole_values`: every pole lies at least 0.4 / 16384 away from every entry of shifts.
All inputs are finite; a program needn't handle non-finite values.
Results may differ from the reference program's by a relative error of at most 0.0003.
Values sent between devices are 32-bit elements; how exact they have to be, the bound alone decides.
A program may use at most 64 MiB of HBM per device.

```python
import jax
import jax.numpy as jnp
from jax import lax

N1 = 8192
K = 16384
SLAB_ROWS = 2048
COLS_DEV = 512
MAX_KEPT = 384


def panel_draw(key, salt):
    base_key = jax.random.fold_in(key, salt)
    row_ramp = 1.0 + 2.0 * jnp.arange(SLAB_ROWS, dtype=jnp.float32) / max(SLAB_ROWS - 1, 1)
    entries = jax.random.normal(base_key, (SLAB_ROWS, N1), jnp.float32)
    return entries * row_ramp[:, None]


def spectrum_draw(key):
    base_key = jax.random.fold_in(key, 101)
    cell_order = jax.random.permutation(jax.random.fold_in(base_key, 1), 4 * K)
    offsets = jax.random.uniform(jax.random.fold_in(base_key, 2), (4 * K,), jnp.float32, 0.2, 0.8)
    cell_values = (cell_order.astype(jnp.float32) + offsets) / K
    return (cell_values[:K].reshape(2, N1), cell_values[K:2 * K])


def deflation_draw(key):
    base_key = jax.random.fold_in(key, 202)
    groups = K // COLS_DEV
    shard_poles = N1 // groups
    counts = jax.random.randint(jax.random.fold_in(base_key, 1), (groups,), COLS_DEV // 8, MAX_KEPT + 1)
    busiest = jax.random.randint(jax.random.fold_in(base_key, 2), (), 0, groups)
    counts = jnp.where(jnp.arange(groups) == busiest, MAX_KEPT, counts)
    scores = jax.random.randint(jax.random.fold_in(base_key, 3), (groups, COLS_DEV), 0, 2 ** 18) * COLS_DEV + jnp.arange(COLS_DEV, dtype=jnp.int32)[None, :]
    rank_order = jnp.argsort(jnp.argsort(scores, axis=1, stable=True), axis=1, stable=True)
    undeflated = rank_order < counts[:, None]
    deflated = jnp.logical_not(undeflated).reshape(-1)
    slot_index = jnp.cumsum(deflated.astype(jnp.int32)) - 1
    whole_kept = jax.random.randint(jax.random.fold_in(base_key, 5), (), 0, groups)
    pole_ids = jnp.arange(K, dtype=jnp.int32)
    pole_owner = pole_ids % N1 // shard_poles
    shuffled = jax.random.permutation(jax.random.fold_in(base_key, 4), K).astype(jnp.int32)
    pole_scores = shuffled + K * (pole_owner == whole_kept).astype(jnp.int32)
    poles_order = jnp.argsort(pole_scores, stable=True).astype(jnp.int32)
    source = jnp.where(deflated, poles_order[jnp.clip(slot_index, 0, K - 1)], K).astype(jnp.int32)
    kept_mask = jnp.ones((K,), jnp.int32).at[source].set(0, mode='drop')
    return (source, kept_mask.reshape(2, N1))


def draw_upper_panel(key, part):
    return panel_draw(key, 11)


def draw_lower_panel(key, part):
    return panel_draw(key, 12)


def draw_pole_values(key, part):
    return spectrum_draw(key)[0]


def draw_shifts(key, part):
    return spectrum_draw(key)[1]


def draw_source(key, part):
    return deflation_draw(key)[0]


def draw_kept_mask(key, part):
    return deflation_draw(key)[1]


def steps_of(stream_key, shape, cuts, low, largest):
    loudness = 1.0
    for dim, shards_of in cuts:
        draws = jax.random.uniform(jax.random.fold_in(jax.random.fold_in(stream_key, 6), dim), (shards_of,), jnp.float32, low / len(cuts), largest / len(cuts))
        loudness = loudness * jnp.repeat(jnp.exp(draws), shape[dim] // shards_of).reshape((-1,) + (1,) * (len(shape) - 1 - dim))
    return loudness


def noise(key, shape, width, reach, split=(), held_as=jnp.bfloat16):
    array = width * jax.random.normal(key, shape, jnp.float32)
    if split:
        array = array * steps_of(key, shape, split, -0.22, 0.18)
    return jnp.clip(array, -reach, reach).astype(held_as)


def setup_inputs(seed: int = 0) -> dict:
    seeds = jax.random.split(jax.random.key(seed), 8)
    upper_panel = draw_upper_panel(jax.random.fold_in(seeds[7], 71), 0)
    lower_panel = draw_lower_panel(jax.random.fold_in(seeds[7], 71), 0)
    pole_values = draw_pole_values(jax.random.fold_in(seeds[7], 71), 0)
    coupling = noise(seeds[3], (2, N1), 1.0, 6.0, ((1, 32),), jnp.float32)
    kept_mask = draw_kept_mask(jax.random.fold_in(seeds[7], 71), 0)
    shifts = draw_shifts(jax.random.fold_in(seeds[7], 71), 0)
    source = draw_source(jax.random.fold_in(seeds[7], 71), 0)
    return dict(upper_panel=upper_panel, lower_panel=lower_panel, pole_values=pole_values, coupling=coupling, kept_mask=kept_mask, shifts=shifts, source=source)


def reference(upper_panel, lower_panel, pole_values, coupling, kept_mask, shifts, source):
    flat_poles = pole_values.reshape(K)
    weighted = (coupling * kept_mask.astype(jnp.float32)).reshape(K)
    block_cols = 512 if K % 512 == 0 else K

    def one_block(begin_at):
        shift_vals = lax.dynamic_slice_in_dim(shifts, begin_at, block_cols)
        targets = lax.dynamic_slice_in_dim(source, begin_at, block_cols)
        cauchy = weighted[:, None] / (flat_poles[:, None] - shift_vals[None, :])
        norm_sums = lax.optimization_barrier(jnp.sum(cauchy * cauchy, axis=0))
        undeflated = targets == K
        one_hot = (jnp.arange(K, dtype=jnp.int32)[:, None] == targets[None, :]).astype(jnp.float32)
        basis_tile = jnp.where(undeflated[None, :], cauchy / jnp.sqrt(norm_sums)[None, :], one_hot)
        upper_acc = jnp.dot(upper_panel, basis_tile[:N1], precision=lax.Precision.HIGHEST, preferred_element_type=jnp.float32)
        lower_acc = jnp.dot(lower_panel, basis_tile[N1:], precision=lax.Precision.HIGHEST, preferred_element_type=jnp.float32)
        return jnp.stack([upper_acc, lower_acc])
    block_starts = jnp.arange(K // block_cols, dtype=jnp.int32) * block_cols
    stacked = lax.map(one_block, block_starts)
    vectors = jnp.transpose(stacked, (1, 2, 0, 3)).reshape(2, SLAB_ROWS, K)
    slab_weight = lax.optimization_barrier(jnp.sum(vectors * vectors, axis=(0, 1))) / (2 * SLAB_ROWS)
    return (vectors, slab_weight)
```

```python
import functools

import jax
import jax.numpy as jnp
from jax import lax
from jax.experimental import pallas as pl
from jax.experimental.pallas import tpu as pltpu
from jax.sharding import PartitionSpec as P

NZ = 8
NY = 4
CHUNKS = 8
LEAD = 2
MESH = pl.DeviceIdType.MESH


def link(src, dst, ssem, rsem, dev):
    return pltpu.make_async_remote_copy(
        src_ref=src, dst_ref=dst, send_sem=ssem, recv_sem=rsem, device_id=dev, device_id_type=MESH
    )


def kernel(
    n_row, child_poles,
    up, lo, poles, coup, mask, shifts, source,
    out, slab,
    abuf, ahl, bh, bl, pbuf, rbuf, fbuf, xbuf, outv,
    pwbuf, ssbuf, nsend, nbuf, pcol, wcol, scale, sq, wbuf,
    own_l, own_s, own_r, s1, a1, sf, af, pws, pwr, sss, ssr, ns, nr,
    rls, rlr, fs, fr, xs, xr, ws, wr, osem,
):
    r = lax.axis_index("row")
    c = lax.axis_index("col")
    k = lax.rem(r, 2)
    r0 = r - k
    y = lax.div(c, NZ)
    z = lax.rem(c, NZ)
    nm = CHUNKS
    half = up.shape[1]
    kb = up.shape[2]
    m2 = 2 * half
    nc = shifts.shape[1]

    def at_z(delta, core):
        return (r0 + core, y * NZ + lax.rem(z + delta + NZ, NZ))

    def at_y(delta, core):
        return (r0 + core, lax.rem(y + delta + NY, NY) * NZ + z)

    def at_row(delta):
        return (lax.rem(r + delta, n_row), c)

    other = (r0 + 1 - k, c)

    barrier = pltpu.get_barrier_semaphore()
    peers = [at_z(d, k) for d in range(1, NZ)] + [at_z(1, 1 - k), at_z(NZ - 1, 1 - k)]
    peers += [at_y(d, q) for d in range(1, NY) for q in (0, 1)]
    peers += [at_row(d) for d in range(1, n_row)]
    for dev in peers:
        pl.semaphore_signal(barrier, inc=1, device_id=dev, device_id_type=MESH)

    pw_rows = lax.broadcasted_iota(jnp.int32, (8, kb), 0)
    pole_row = jnp.broadcast_to(poles[pl.ds(k, 1), :], (8, kb))
    weight_row = jnp.broadcast_to(
        coup[pl.ds(k, 1), :] * mask[pl.ds(k, 1), :].astype(jnp.float32), (8, kb)
    )
    pwbuf[0] = jnp.where(pw_rows == 0, pole_row, weight_row)
    ssbuf[0, 0] = jnp.broadcast_to(shifts[...], (8, nc))
    ssbuf[0, 1] = jnp.broadcast_to(source[...].astype(jnp.float32), (8, nc))
    nsend[...] = jnp.zeros_like(nsend)
    sq[...] = jnp.zeros_like(sq)

    pl.semaphore_wait(barrier, len(peers))

    panels = (up, lo)

    def own_copies(m):
        return [
            link(
                panels[child].at[m], abuf.at[NZ - 1 if step == 1 else 1, m, k],
                s1.at[d, m, child], a1.at[d, m, k], at_z(step, child),
            )
            for d, step in ((0, 1), (1, NZ - 1))
            for child in (0, 1)
        ]

    def first_wait(d, m, o):
        dst = abuf.at[NZ - 1 if d == 0 else 1, m, o]
        return link(dst, dst, s1.at[d, m, 0], a1.at[d, m, o], other)

    def forward(d, m, stage):
        step = 1 if d == 0 else NZ - 1
        src_rel = NZ - 1 - stage if d == 0 else 1 + stage
        dst_rel = src_rel - 1 if d == 0 else src_rel + 1
        if stage < 2:
            src, dst = abuf.at[src_rel, m], abuf.at[dst_rel, m]
        else:
            src, dst = abuf.at[src_rel, m, d], abuf.at[dst_rel, m, d]
        return link(src, dst, sf.at[d, m, stage], af.at[d, m, stage], at_z(step, k))

    for dlt in range(1, NZ):
        link(pwbuf.at[0], pwbuf.at[NZ - dlt], pws.at[dlt], pwr.at[NZ - dlt], at_z(dlt, k)).start()
    for dlt in range(1, NY):
        link(ssbuf.at[0], ssbuf.at[NY - dlt], sss.at[dlt], ssr.at[NY - dlt], at_y(dlt, k)).start()
    for m in range(LEAD + 1):
        for copy in own_copies(m):
            copy.start()
    for child in (0, 1):
        local = pltpu.make_async_copy(panels[child], abuf.at[0, :, k], own_l)
        across = link(panels[child], abuf.at[0, :, k], own_s, own_r, other)

        @pl.when(k == child)
        def _():
            local.start()

        @pl.when(k != child)
        def _():
            across.start()

    for dlt in range(1, NY):
        link(ssbuf.at[0], ssbuf.at[dlt], sss.at[dlt], ssr.at[dlt], other).wait_recv()
    for dlt in range(1, NZ):
        link(pwbuf.at[0], pwbuf.at[dlt], pws.at[dlt], pwr.at[dlt], other).wait_recv()

    block_rows = min(64, kb)

    def basis_block(rel):
        pw = pwbuf[rel]
        pcol[...] = jnp.broadcast_to(pw[0:1, :], (128, kb)).T
        wcol[...] = jnp.broadcast_to(pw[1:2, :], (128, kb)).T
        first = k * child_poles + (y * NZ + lax.rem(z + rel, NZ)) * kb

        @pl.loop(0, NY * (nc // 128))
        def _(tile):
            dest = lax.div(tile, nc // 128)
            lane = pl.multiple_of(lax.rem(tile, nc // 128) * 128, 128)
            shift = ssbuf[dest, 0, :, pl.ds(lane, 128)]
            named = ssbuf[dest, 1, :, pl.ds(lane, 128)]
            kept = named == 2.0 * child_poles
            total = nsend[dest, :, pl.ds(lane, 128)]
            for rb in range(kb // block_rows):
                rows = pl.ds(rb * block_rows, block_rows)
                shape = (block_rows // 8, 8, 128)
                pole = pcol[rows, :].reshape(shape)
                weight = wcol[rows, :].reshape(shape)
                cauchy = weight / (pole - shift[None])
                total = total + jnp.sum(cauchy * cauchy, axis=0)
                ids = (
                    lax.broadcasted_iota(jnp.int32, shape, 0) * 8
                    + lax.broadcasted_iota(jnp.int32, shape, 1)
                    + (first + rb * block_rows)
                ).astype(jnp.float32)
                hot = jnp.where(ids == named[None], 1.0, 0.0)
                value = jnp.where(kept[None], cauchy, hot).reshape(block_rows, 128)
                high = value.astype(jnp.bfloat16)
                low = (value - high.astype(jnp.float32)).astype(jnp.bfloat16)
                at = pl.ds(pl.multiple_of(rel * kb + rb * block_rows, block_rows), block_rows)
                bh[dest, at, pl.ds(lane, 128)] = high
                bl[dest, at, pl.ds(lane, 128)] = low
            nsend[dest, :, pl.ds(lane, 128)] = total

    def norm_copies():
        copies = []
        for dlt in range(NY):
            for q in (0, 1):
                slot = (NY - dlt) % NY
                copies.append((dlt, q, link(
                    nsend.at[dlt], nbuf.at[slot, k], ns.at[dlt, q], nr.at[slot, k], at_y(dlt, q)
                )))
        return copies

    def relay(m, d):
        step = 1 if d == 0 else NY - 1
        return link(pbuf.at[2, m, d], rbuf.at[d, m], rls.at[d, m], rlr.at[d, m], at_y(step, k))

    def final(m, d, o):
        step = 1 if d == 0 else NY - 1
        return link(
            pbuf.at[step, m, o], fbuf.at[k, d, m], fs.at[d, m, o], fr.at[k, d, m], at_y(step, o)
        )

    def cross(m):
        return link(pbuf.at[0, m, 1 - k], xbuf.at[m], xs.at[m], xr.at[m], other)

    def multiply(m):
        for rel in range(NZ):
            a = abuf[rel, m].reshape(m2, kb)
            high = a.astype(jnp.bfloat16)
            low = (a - high.astype(jnp.float32)).astype(jnp.bfloat16)
            ahl[0:m2, rel * kb : (rel + 1) * kb] = high
            ahl[m2 : 2 * m2, rel * kb : (rel + 1) * kb] = low
        for dest in (2, 1, 3, 0):
            both = jnp.dot(ahl[...], bh[dest], preferred_element_type=jnp.float32)
            rest = jnp.dot(ahl[0:m2, :], bl[dest], preferred_element_type=jnp.float32)
            pbuf[dest, m] = (both[0:m2] + (both[m2:] + rest)).reshape(2, half, nc)
            if dest == 2:
                relay(m, 0).start()
                relay(m, 1).start()
            elif dest == 1:
                final(m, 0, 1).start()
            elif dest == 3:
                final(m, 1, 0).start()
            else:
                cross(m).start()

    def add_relays(m):
        relay(m, 0).wait_recv()
        pbuf[1, m, 0] = pbuf[1, m, 0] + rbuf[0, m]
        final(m, 0, 0).start()
        relay(m, 1).wait_recv()
        pbuf[3, m, 1] = pbuf[3, m, 1] + rbuf[1, m]
        final(m, 1, 1).start()

    def finish(m):
        for child in (0, 1):
            for d in (0, 1):
                dst = fbuf.at[child, d, m]
                link(dst, dst, fs.at[d, m, 0], fr.at[child, d, m], other).wait_recv()
        cross(m).wait_recv()
        factor = scale[0:1, :]
        mine = (pbuf[0, m, k] + (fbuf[k, 0, m] + fbuf[k, 1, m])) * factor
        theirs = (xbuf[m] + (fbuf[1 - k, 0, m] + fbuf[1 - k, 1, m])) * factor
        outv[k, m] = mine
        outv[1 - k, m] = theirs
        squares = (mine * mine + theirs * theirs).reshape(half // 8, 8, nc)
        sq[...] = sq[...] + jnp.sum(squares, axis=0)
        pltpu.make_async_copy(outv.at[:, m], out.at[:, m], osem.at[m]).start()

    def within(m):
        return jnp.logical_and(m >= 0, m < nm)

    @pl.loop(0, nm + 6)
    def _(t):
        @pl.when(within(t - 4))
        def _():
            for d in (0, 1):
                forward(d, t - 4, 2).wait_recv()

        for stage in (2, 1):
            @pl.when(within(t - 1 - stage))
            def _():
                for d in (0, 1):
                    forward(d, t - 1 - stage, stage - 1).wait_recv()
                    forward(d, t - 1 - stage, stage).start()

        @pl.when(within(t - 1))
        def _():
            for d in (0, 1):
                for o in (0, 1):
                    first_wait(d, t - 1, o).wait_recv()
                forward(d, t - 1, 0).start()

        @pl.when(t + LEAD + 1 < nm)
        def _():
            for copy in own_copies(t + LEAD + 1):
                copy.start()

        @pl.when(t < 4)
        def _():
            basis_block(2 * t)
            basis_block(2 * t + 1)

        @pl.when(t == 3)
        def _():
            pltpu.make_async_copy(up, abuf.at[0, :, k], own_l).wait()
            link(up, abuf.at[0, :, 1 - k], own_s, own_r, other).wait_recv()
            for dlt, q, copy in norm_copies():
                if dlt > 0:
                    copy.start()
                else:
                    @pl.when(k != q)
                    def _():
                        copy.start()
            nbuf[0, k] = nsend[0]

        @pl.when(within(t - 4))
        def _():
            multiply(t - 4)

        @pl.when(within(t - 5))
        def _():
            add_relays(t - 5)

        @pl.when(t == 6)
        def _():
            total = jnp.zeros((8, nc), jnp.float32)
            for slot in range(NY):
                for q in (0, 1):
                    dst = nbuf.at[slot, q]
                    incoming = link(dst, dst, ns.at[1, 0], nr.at[slot, q], other)
                    if slot > 0:
                        incoming.wait_recv()
                    else:
                        @pl.when(k != q)
                        def _():
                            incoming.wait_recv()
            for slot in range(NY):
                for q in (0, 1):
                    total = total + nbuf[slot, q]
            sums = jnp.sum(total, axis=0, keepdims=True)
            kept = ssbuf[0, 1, 0:1, :] == 2.0 * child_poles
            scale[...] = jnp.broadcast_to(
                jnp.where(kept, 1.0 / jnp.sqrt(sums), 1.0), (8, nc)
            )

        @pl.when(within(t - 6))
        def _():
            finish(t - 6)

    wbuf[0] = sq[...]
    for dlt in range(1, n_row):
        link(wbuf.at[0], wbuf.at[n_row - dlt], ws.at[dlt], wr.at[n_row - dlt], at_row(dlt)).start()

    for dlt in range(1, NZ):
        link(pwbuf.at[0], pwbuf.at[dlt], pws.at[dlt], pwr.at[dlt], other).wait_send()
    for dlt in range(1, NY):
        link(ssbuf.at[0], ssbuf.at[dlt], sss.at[dlt], ssr.at[dlt], other).wait_send()
    link(up, abuf.at[0, :, k], own_s, own_r, other).wait_send()
    for dlt, q, copy in norm_copies():
        if dlt > 0:
            copy.wait_send()
        else:
            @pl.when(k != q)
            def _():
                copy.wait_send()

    @pl.loop(0, nm)
    def _(m):
        for copy in own_copies(m):
            copy.wait_send()
        for d in (0, 1):
            for stage in (0, 1, 2):
                forward(d, m, stage).wait_send()
            relay(m, d).wait_send()
            final(m, d, 0).wait_send()
            final(m, d, 1).wait_send()
        cross(m).wait_send()
        pltpu.make_async_copy(outv.at[:, m], out.at[:, m], osem.at[m]).wait()

    weight_sum = wbuf[0]
    for dlt in range(1, n_row):
        link(wbuf.at[0], wbuf.at[dlt], ws.at[dlt], wr.at[dlt], other).wait_recv()
    for dlt in range(1, n_row):
        weight_sum = weight_sum + wbuf[dlt]
    rows_all = 2 * n_row * nm * half
    slab[...] = jnp.sum(weight_sum, axis=0, keepdims=True) * (1.0 / rows_all)
    for dlt in range(1, n_row):
        link(wbuf.at[0], wbuf.at[dlt], ws.at[dlt], wr.at[dlt], other).wait_send()


def local(n_row, upper_panel, lower_panel, pole_values, coupling, kept_mask, shifts, source):
    rows, kb = upper_panel.shape
    nc = shifts.shape[0]
    nm = CHUNKS
    half = rows // nm
    m2 = 2 * half
    child_poles = NZ * NY * kb
    kpart = NZ * kb
    f32 = jnp.float32
    dma = pltpu.SemaphoreType.DMA
    vmem = pl.BlockSpec(memory_space=pltpu.VMEM)
    hbm = pl.BlockSpec(memory_space=pl.ANY)
    out, slab = pl.pallas_call(
        functools.partial(kernel, n_row, child_poles),
        out_shape=(
            jax.ShapeDtypeStruct((2, nm, half, nc), f32),
            jax.ShapeDtypeStruct((1, nc), f32),
        ),
        in_specs=[hbm, hbm, vmem, vmem, vmem, vmem, vmem],
        out_specs=(hbm, vmem),
        scratch_shapes=[
            pltpu.VMEM((NZ, nm, 2, half, kb), f32),
            pltpu.VMEM((2 * m2, kpart), jnp.bfloat16),
            pltpu.VMEM((NY, kpart, nc), jnp.bfloat16),
            pltpu.VMEM((NY, kpart, nc), jnp.bfloat16),
            pltpu.VMEM((NY, nm, 2, half, nc), f32),
            pltpu.VMEM((2, nm, half, nc), f32),
            pltpu.VMEM((2, 2, nm, half, nc), f32),
            pltpu.VMEM((nm, half, nc), f32),
            pltpu.VMEM((2, nm, half, nc), f32),
            pltpu.VMEM((NZ, 8, kb), f32),
            pltpu.VMEM((NY, 2, 8, nc), f32),
            pltpu.VMEM((NY, 8, nc), f32),
            pltpu.VMEM((NY, 2, 8, nc), f32),
            pltpu.VMEM((kb, 128), f32),
            pltpu.VMEM((kb, 128), f32),
            pltpu.VMEM((8, nc), f32),
            pltpu.VMEM((8, nc), f32),
            pltpu.VMEM((n_row, 8, nc), f32),
            dma, dma, dma,
            dma((2, nm, 2)), dma((2, nm, 2)),
            dma((2, nm, 3)), dma((2, nm, 3)),
            dma((NZ,)), dma((NZ,)),
            dma((NY,)), dma((NY,)),
            dma((NY, 2)), dma((NY, 2)),
            dma((2, nm)), dma((2, nm)),
            dma((2, nm, 2)), dma((2, 2, nm)),
            dma((nm,)), dma((nm,)),
            dma((n_row,)), dma((n_row,)),
            dma((nm,)),
        ],
        compiler_params=pltpu.CompilerParams(
            collective_id=0, has_side_effects=True, vmem_limit_bytes=60 * 1024 * 1024
        ),
    )(
        upper_panel.reshape(nm, half, kb),
        lower_panel.reshape(nm, half, kb),
        pole_values,
        coupling,
        kept_mask,
        shifts.reshape(1, nc),
        source.reshape(1, nc),
    )
    return out.reshape(2, rows, nc), slab.reshape(nc)


def solution(mesh):
    in_specs = (
        P("row", "col"),
        P("row", "col"),
        P(None, "col"),
        P(None, "col"),
        P(None, "col"),
        P("col"),
        P("col"),
    )
    out_specs = (P(None, "row", "col"), P("col"))
    body = functools.partial(local, mesh.shape["row"])
    return jax.shard_map(body, mesh=mesh, in_specs=in_specs, out_specs=out_specs, check_vma=False)
```

```python
import functools

import jax
import jax.numpy as jnp
from jax import lax
from jax.experimental import pallas as pl
from jax.experimental.pallas import tpu as pltpu
from jax.sharding import PartitionSpec as P

NZ = 8
NY = 4
CHUNKS = 8
LEAD = 3
MESH = pl.DeviceIdType.MESH


def link(src, dst, ssem, rsem, dev):
    return pltpu.make_async_remote_copy(
        src_ref=src, dst_ref=dst, send_sem=ssem, recv_sem=rsem, device_id=dev, device_id_type=MESH
    )


def kernel(
    n_row, child_poles,
    up, lo, poles, coup, mask, shifts, source,
    out, slab,
    abuf, ahl, atail, bh, bl, pbuf, rbuf, fbuf, outv,
    pwbuf, ssbuf, nsend, nbuf, pcol, wcol, scale, sq, wbuf,
    own_l, own_s, own_r, s1, a1, sf, af, pws, pwr, sss, ssr, ns, nr,
    rls, rlr, fs, fr, xs, ws, wr, osem,
):
    r = lax.axis_index("row")
    c = lax.axis_index("col")
    k = lax.rem(r, 2)
    r0 = r - k
    y = lax.div(c, NZ)
    z = lax.rem(c, NZ)
    nm = CHUNKS
    half = up.shape[1]
    kb = up.shape[2]
    m2 = 2 * half
    nc = shifts.shape[1]

    def at_z(delta, core):
        return (r0 + core, y * NZ + lax.rem(z + delta + NZ, NZ))

    def at_y(delta, core):
        return (r0 + core, lax.rem(y + delta + NY, NY) * NZ + z)

    def at_row(delta):
        return (lax.rem(r + delta, n_row), c)

    other = (r0 + 1 - k, c)

    barrier = pltpu.get_barrier_semaphore()
    peers = [at_z(d, k) for d in range(1, NZ)] + [at_z(1, 1 - k), at_z(NZ - 1, 1 - k)]
    peers += [at_y(d, q) for d in range(1, NY) for q in (0, 1)]
    peers += [at_row(d) for d in range(1, n_row)]
    for dev in peers:
        pl.semaphore_signal(barrier, inc=1, device_id=dev, device_id_type=MESH)

    pw_rows = lax.broadcasted_iota(jnp.int32, (8, kb), 0)
    pole_row = jnp.broadcast_to(poles[pl.ds(k, 1), :], (8, kb))
    weight_row = jnp.broadcast_to(
        coup[pl.ds(k, 1), :] * mask[pl.ds(k, 1), :].astype(jnp.float32), (8, kb)
    )
    pwbuf[0] = jnp.where(pw_rows == 0, pole_row, weight_row)
    ssbuf[0, 0] = jnp.broadcast_to(shifts[...], (8, nc))
    ssbuf[0, 1] = jnp.broadcast_to(source[...].astype(jnp.float32), (8, nc))
    nsend[...] = jnp.zeros_like(nsend)
    sq[...] = jnp.zeros_like(sq)

    pl.semaphore_wait(barrier, len(peers))

    panels = (up, lo)

    def own_copies(m):
        return [
            link(
                panels[child].at[m], abuf.at[NZ - 1 if step == 1 else 1, m, k],
                s1.at[d, lax.rem(m, 4), child], a1.at[d, m], at_z(step, child),
            )
            for d, step in ((0, 1), (1, NZ - 1))
            for child in (0, 1)
        ]

    def first_wait(d, m):
        dst = abuf.at[NZ - 1 if d == 0 else 1, m]
        return link(dst, dst, s1.at[d, 0, 0], a1.at[d, m], other)

    def forward(d, m, stage):
        step = 1 if d == 0 else NZ - 1
        src_rel = NZ - 1 - stage if d == 0 else 1 + stage
        dst_rel = src_rel - 1 if d == 0 else src_rel + 1
        if stage < 2:
            src, dst = abuf.at[src_rel, m], abuf.at[dst_rel, m]
        else:
            src, dst = abuf.at[src_rel, m, d], abuf.at[dst_rel, m, d]
        return link(src, dst, sf.at[d, lax.rem(m, 2), stage], af.at[d, m, stage], at_z(step, k))

    def push(d, m, stage):
        @pl.when(m >= 2)
        def _():
            forward(d, m - 2, stage).wait_send()

        forward(d, m, stage).start()

    for dlt in range(1, NZ):
        link(pwbuf.at[0], pwbuf.at[NZ - dlt], pws, pwr, at_z(dlt, k)).start()
    for dlt in range(1, NY):
        link(ssbuf.at[0], ssbuf.at[NY - dlt], sss, ssr, at_y(dlt, k)).start()
    for m in range(LEAD):
        for copy in own_copies(m):
            copy.start()
    for child in (0, 1):
        local = pltpu.make_async_copy(panels[child], abuf.at[0, :, k], own_l)
        across = link(panels[child], abuf.at[0, :, k], own_s, own_r, other)

        @pl.when(k == child)
        def _():
            local.start()

        @pl.when(k != child)
        def _():
            across.start()

    all_shifts = link(ssbuf.at[1:NY], ssbuf.at[1:NY], sss, ssr, other)
    all_poles = link(pwbuf.at[1:NZ], pwbuf.at[1:NZ], pws, pwr, other)
    all_shifts.wait_recv()
    block_rows = min(64, kb)

    def basis_block(pos):
        rel = pos + lax.div(pos, 4) - 4 * lax.div(pos, NZ - 1)
        pw = pwbuf[rel]
        pcol[...] = jnp.broadcast_to(pw[0:1, :], (128, kb)).T
        wcol[...] = jnp.broadcast_to(pw[1:2, :], (128, kb)).T
        first = k * child_poles + (y * NZ + lax.rem(z + rel, NZ)) * kb

        @pl.loop(0, NY * (nc // 128))
        def _(tile):
            dest = lax.div(tile, nc // 128)
            lane = pl.multiple_of(lax.rem(tile, nc // 128) * 128, 128)
            shift = ssbuf[dest, 0, :, pl.ds(lane, 128)]
            named = ssbuf[dest, 1, :, pl.ds(lane, 128)]
            kept = named == 2.0 * child_poles
            total = nsend[dest, :, pl.ds(lane, 128)]
            for rb in range(kb // block_rows):
                rows = pl.ds(rb * block_rows, block_rows)
                shape = (block_rows // 8, 8, 128)
                pole = pcol[rows, :].reshape(shape)
                weight = wcol[rows, :].reshape(shape)
                cauchy = weight / (pole - shift[None])
                total = total + jnp.sum(cauchy * cauchy, axis=0)
                ids = (
                    lax.broadcasted_iota(jnp.int32, shape, 0) * 8
                    + lax.broadcasted_iota(jnp.int32, shape, 1)
                    + (first + rb * block_rows)
                ).astype(jnp.float32)
                hot = jnp.where(ids == named[None], 1.0, 0.0)
                value = jnp.where(kept[None], cauchy, hot).reshape(block_rows, 128)
                high = value.astype(jnp.bfloat16)
                low = (value - high.astype(jnp.float32)).astype(jnp.bfloat16)
                at = pl.ds(pl.multiple_of(pos * kb + rb * block_rows, block_rows), block_rows)
                bh[dest, at, pl.ds(lane, 128)] = high
                bl[dest, at, pl.ds(lane, 128)] = low
            nsend[dest, :, pl.ds(lane, 128)] = total

    def send_norms():
        for dlt in range(NY):
            for flip in (0, 1):
                slot = 2 * ((NY - dlt) % NY) + flip
                if slot > 0:
                    core = 1 - k if flip else k
                    link(nsend.at[dlt], nbuf.at[slot], ns, nr, at_y(dlt, core)).start()

    all_norms = link(nbuf.at[1 : 2 * NY], nbuf.at[1 : 2 * NY], ns, nr, other)

    def relay(m, d):
        step = 1 if d == 0 else NY - 1
        return link(
            pbuf.at[2, m, d], rbuf.at[d, m], rls.at[d, lax.rem(m, 2)], rlr.at[d, m], at_y(step, k)
        )

    def final(m, d, o):
        step = 1 if d == 0 else NY - 1
        return link(
            pbuf.at[step, m, o], fbuf.at[m, 2 * k + d], fs.at[d, lax.rem(m, 2), o], fr.at[m],
            at_y(step, o),
        )

    def cross(m):
        return link(pbuf.at[0, m, 1 - k], fbuf.at[m, 4], xs.at[lax.rem(m, 2)], fr.at[m], other)

    def split(rel, m):
        a = abuf[rel, m].reshape(m2, kb)
        high = a.astype(jnp.bfloat16)
        return high, (a - high.astype(jnp.float32)).astype(jnp.bfloat16)

    def split_early(m):
        for pos in range(NZ - 1):
            high, low = split(pos + pos // 4, m)
            ahl[0:m2, pos * kb : (pos + 1) * kb] = high
            ahl[m2 : 2 * m2, pos * kb : (pos + 1) * kb] = low

    early = (NZ - 1) * kb

    def product(a, dest, first, size):
        rows = slice(first, first + size)
        both = jnp.dot(a[...], bh[dest, rows, :], preferred_element_type=jnp.float32)
        rest = jnp.dot(a[0:m2, :], bl[dest, rows, :], preferred_element_type=jnp.float32)
        return (both[0:m2] + (both[m2:] + rest)).reshape(2, half, nc)

    def multiply_early(m, dest):
        pbuf[dest, m] = product(ahl, dest, 0, early)

    def multiply_late(m):
        atail[0:m2, :], atail[m2 : 2 * m2, :] = split(4, m)
        for dest in (2, 1, 3, 0):
            pbuf[dest, m] = pbuf[dest, m] + product(atail, dest, early, kb)
            if dest == 2:
                relay(m, 0).start()
                relay(m, 1).start()
            elif dest == 1:
                final(m, 0, 1).start()
            elif dest == 3:
                final(m, 1, 0).start()
            else:
                cross(m).start()

    def sums_sent(m):
        for d in (0, 1):
            relay(m, d).wait_send()
            final(m, d, 1 - d).wait_send()
        cross(m).wait_send()

    def added_sent(m):
        for d in (0, 1):
            final(m, d, d).wait_send()

    def add_relays(m):
        @pl.when(m >= 2)
        def _():
            added_sent(m - 2)

        relay(m, 0).wait_recv()
        pbuf[1, m, 0] = pbuf[1, m, 0] + rbuf[0, m]
        final(m, 0, 0).start()
        relay(m, 1).wait_recv()
        pbuf[3, m, 1] = pbuf[3, m, 1] + rbuf[1, m]
        final(m, 1, 1).start()

    def store(m):
        return pltpu.make_async_copy(outv.at[:, m], out.at[:, m], osem.at[lax.rem(m, 2)])

    def finish(m):
        link(fbuf.at[m], fbuf.at[m], xs.at[0], fr.at[m], other).wait_recv()
        factor = scale[0:1, :]
        mine = (pbuf[0, m, k] + (fbuf[m, 2 * k] + fbuf[m, 2 * k + 1])) * factor
        theirs = (fbuf[m, 4] + (fbuf[m, 2 - 2 * k] + fbuf[m, 3 - 2 * k])) * factor
        outv[k, m] = mine
        outv[1 - k, m] = theirs
        squares = (mine * mine + theirs * theirs).reshape(half // 8, 8, nc)
        sq[...] = sq[...] + jnp.sum(squares, axis=0)
        @pl.when(m >= 2)
        def _():
            store(m - 2).wait()

        store(m).start()

    def within(m):
        return jnp.logical_and(m >= 0, m < nm)

    @pl.loop(0, nm + 6)
    def _(t):
        @pl.when(within(t - 4))
        def _():
            for d in (0, 1):
                forward(d, t - 4, 2).wait_recv()
            @pl.when(t >= 6)
            def _():
                sums_sent(t - 6)
            multiply_late(t - 4)

        @pl.when(t + LEAD < nm)
        def _():
            @pl.when(t + LEAD >= 4)
            def _():
                for copy in own_copies(t + LEAD - 4):
                    copy.wait_send()
            for copy in own_copies(t + LEAD):
                copy.start()

        @pl.when(t < 3)
        def _():
            basis_block(3 * t)

        @pl.when(t == 0)
        def _():
            all_poles.wait_recv()

        @pl.when(within(t))
        def _():
            for d in (0, 1):
                first_wait(d, t).wait_recv()
                push(d, t, 0)

        @pl.when(t < 3)
        def _():
            basis_block(3 * t + 1)

        @pl.when(within(t - 3))
        def _():
            split_early(t - 3)
            multiply_early(t - 3, 2)

        @pl.when(within(t - 1))
        def _():
            for d in (0, 1):
                forward(d, t - 1, 0).wait_recv()
                push(d, t - 1, 1)

        @pl.when(t < 2)
        def _():
            basis_block(3 * t + 2)

        @pl.when(within(t - 3))
        def _():
            multiply_early(t - 3, 1)

        @pl.when(within(t - 2))
        def _():
            for d in (0, 1):
                forward(d, t - 2, 1).wait_recv()
                push(d, t - 2, 2)

        @pl.when(within(t - 3))
        def _():
            multiply_early(t - 3, 3)
            multiply_early(t - 3, 0)

        @pl.when(t == 2)
        def _():
            pltpu.make_async_copy(up, abuf.at[0, :, k], own_l).wait()
            link(up, abuf.at[0, :, 1 - k], own_s, own_r, other).wait_recv()
            send_norms()
            nbuf[0] = nsend[0]

        @pl.when(within(t - 5))
        def _():
            add_relays(t - 5)

        @pl.when(t == 6)
        def _():
            all_norms.wait_recv()
            total = nbuf[0]
            for slot in range(1, 2 * NY):
                total = total + nbuf[slot]
            sums = jnp.sum(total, axis=0, keepdims=True)
            kept = ssbuf[0, 1, 0:1, :] == 2.0 * child_poles
            scale[...] = jnp.broadcast_to(
                jnp.where(kept, 1.0 / jnp.sqrt(sums), 1.0), (8, nc)
            )

        @pl.when(within(t - 6))
        def _():
            finish(t - 6)

    wbuf[0] = jnp.sum(sq[...], axis=0, keepdims=True)
    for dlt in range(1, n_row):
        link(wbuf.at[0], wbuf.at[n_row - dlt], ws, wr, at_row(dlt)).start()
    all_weights = link(wbuf.at[1:n_row], wbuf.at[1:n_row], ws, wr, other)

    all_poles.wait_send()
    all_shifts.wait_send()
    link(up, abuf.at[0, :, k], own_s, own_r, other).wait_send()
    all_norms.wait_send()

    for m in range(nm - 4, nm):
        for copy in own_copies(m):
            copy.wait_send()
    for m in range(nm - 2, nm):
        for d in (0, 1):
            for stage in (0, 1, 2):
                forward(d, m, stage).wait_send()
        sums_sent(m)
        added_sent(m)
        store(m).wait()

    weight_sum = wbuf[0]
    all_weights.wait_recv()
    for dlt in range(1, n_row):
        weight_sum = weight_sum + wbuf[dlt]
    rows_all = 2 * n_row * nm * half
    slab[...] = weight_sum * (1.0 / rows_all)
    all_weights.wait_send()


def local(n_row, upper_panel, lower_panel, pole_values, coupling, kept_mask, shifts, source):
    rows, kb = upper_panel.shape
    nc = shifts.shape[0]
    nm = CHUNKS
    half = rows // nm
    m2 = 2 * half
    child_poles = NZ * NY * kb
    kpart = NZ * kb
    f32 = jnp.float32
    dma = pltpu.SemaphoreType.DMA
    vmem = pl.BlockSpec(memory_space=pltpu.VMEM)
    hbm = pl.BlockSpec(memory_space=pl.ANY)
    out, slab = pl.pallas_call(
        functools.partial(kernel, n_row, child_poles),
        out_shape=(
            jax.ShapeDtypeStruct((2, nm, half, nc), f32),
            jax.ShapeDtypeStruct((1, nc), f32),
        ),
        in_specs=[hbm, hbm, vmem, vmem, vmem, vmem, vmem],
        out_specs=(hbm, vmem),
        scratch_shapes=[
            pltpu.VMEM((NZ, nm, 2, half, kb), f32),
            pltpu.VMEM((2 * m2, kpart - kb), jnp.bfloat16),
            pltpu.VMEM((2 * m2, kb), jnp.bfloat16),
            pltpu.VMEM((NY, kpart, nc), jnp.bfloat16),
            pltpu.VMEM((NY, kpart, nc), jnp.bfloat16),
            pltpu.VMEM((NY, nm, 2, half, nc), f32),
            pltpu.VMEM((2, nm, half, nc), f32),
            pltpu.VMEM((nm, 5, half, nc), f32),
            pltpu.VMEM((2, nm, half, nc), f32),
            pltpu.VMEM((NZ, 8, kb), f32),
            pltpu.VMEM((NY, 2, 8, nc), f32),
            pltpu.VMEM((NY, 8, nc), f32),
            pltpu.VMEM((2 * NY, 8, nc), f32),
            pltpu.VMEM((kb, 128), f32),
            pltpu.VMEM((kb, 128), f32),
            pltpu.VMEM((8, nc), f32),
            pltpu.VMEM((8, nc), f32),
            pltpu.VMEM((n_row, 1, nc), f32),
            dma, dma, dma,
            dma((2, 4, 2)), dma((2, nm)),
            dma((2, 2, 3)), dma((2, nm, 3)),
            dma, dma, dma, dma, dma, dma,
            dma((2, 2)), dma((2, nm)),
            dma((2, 2, 2)), dma((nm,)),
            dma((2,)), dma, dma, dma((2,)),
        ],
        compiler_params=pltpu.CompilerParams(
            collective_id=0, has_side_effects=True, vmem_limit_bytes=60 * 1024 * 1024
        ),
    )(
        upper_panel.reshape(nm, half, kb),
        lower_panel.reshape(nm, half, kb),
        pole_values,
        coupling,
        kept_mask,
        shifts.reshape(1, nc),
        source.reshape(1, nc),
    )
    return out.reshape(2, rows, nc), slab.reshape(nc)


def solution(mesh):
    in_specs = (
        P("row", "col"),
        P("row", "col"),
        P(None, "col"),
        P(None, "col"),
        P(None, "col"),
        P("col"),
        P("col"),
    )
    out_specs = (P(None, "row", "col"), P("col"))
    body = functools.partial(local, mesh.shape["row"])
    return jax.shard_map(body, mesh=mesh, in_specs=in_specs, out_specs=out_specs, check_vma=False)
```

```python
import functools

import jax
import jax.numpy as jnp
from jax import lax
from jax.experimental import pallas as pl
from jax.experimental.pallas import tpu as pltpu
from jax.sharding import PartitionSpec as P

NZ = 8
NY = 4
CHUNKS = 8
LEAD = 3
MESH = pl.DeviceIdType.MESH


def link(src, dst, ssem, rsem, dev):
    return pltpu.make_async_remote_copy(
        src_ref=src, dst_ref=dst, send_sem=ssem, recv_sem=rsem, device_id=dev, device_id_type=MESH
    )


def kernel(
    n_row, child_poles,
    up, lo, poles_in, coup_in, mask_in, shifts_in, source_in,
    out, slab,
    abuf, ahl, atail, bh, bl, pbuf, rbuf, fbuf,
    pwbuf, ssbuf, nsend, nbuf, pcol, wcol, scale, sq, wbuf,
    poles, coup, mask, shifts, source,
    own_l, own_s, own_r, s1, a1, sf, af, pws, pwr, sss, ssr, ns, nr,
    rls, rlr, fs, fr, xs, ws, wr, isem,
):
    r = lax.axis_index("row")
    c = lax.axis_index("col")
    k = lax.rem(r, 2)
    r0 = r - k
    y = lax.div(c, NZ)
    z = lax.rem(c, NZ)
    nm = CHUNKS
    half = up.shape[1]
    kb = up.shape[2]
    m2 = 2 * half
    nc = shifts.shape[1]
    fetches = [
        pltpu.make_async_copy(given, held, isem.at[n])
        for n, (given, held) in enumerate(
            zip(
                (poles_in, coup_in, mask_in, shifts_in, source_in),
                (poles, coup, mask, shifts, source),
            )
        )
    ]
    for fetch in fetches:
        fetch.start()

    def at_z(delta, core):
        return (r0 + core, y * NZ + lax.rem(z + delta + NZ, NZ))

    def at_y(delta, core):
        return (r0 + core, lax.rem(y + delta + NY, NY) * NZ + z)

    def at_row(delta):
        return (lax.rem(r + delta, n_row), c)

    other = (r0 + 1 - k, c)

    barrier = pltpu.get_barrier_semaphore()
    peers = [at_z(d, k) for d in range(1, NZ)] + [at_z(1, 1 - k), at_z(NZ - 1, 1 - k)]
    peers += [at_y(d, q) for d in range(1, NY) for q in (0, 1)]
    peers += [at_row(d) for d in range(1, n_row)]
    for dev in peers:
        pl.semaphore_signal(barrier, inc=1, device_id=dev, device_id_type=MESH)

    for fetch in fetches:
        fetch.wait()
    pw_rows = lax.broadcasted_iota(jnp.int32, (8, kb), 0)
    pole_row = jnp.broadcast_to(poles[pl.ds(k, 1), :], (8, kb))
    weight_row = jnp.broadcast_to(
        coup[pl.ds(k, 1), :] * mask[pl.ds(k, 1), :].astype(jnp.float32), (8, kb)
    )
    pwbuf[0] = jnp.where(pw_rows == 0, pole_row, weight_row)
    ssbuf[0, 0] = jnp.broadcast_to(shifts[...], (8, nc))
    ssbuf[0, 1] = jnp.broadcast_to(source[...].astype(jnp.float32), (8, nc))
    nsend[...] = jnp.zeros_like(nsend)
    sq[...] = jnp.zeros_like(sq)

    pl.semaphore_wait(barrier, len(peers))

    panels = (up, lo)

    def own_copies(m):
        return [
            link(
                panels[child].at[m], abuf.at[NZ - 1 if step == 1 else 1, m, k],
                s1.at[d, lax.rem(m, 4), child], a1.at[d, m], at_z(step, child),
            )
            for d, step in ((0, 1), (1, NZ - 1))
            for child in (0, 1)
        ]

    def first_wait(d, m):
        dst = abuf.at[NZ - 1 if d == 0 else 1, m]
        return link(dst, dst, s1.at[d, 0, 0], a1.at[d, m], other)

    def forward(d, m, stage):
        step = 1 if d == 0 else NZ - 1
        src_rel = NZ - 1 - stage if d == 0 else 1 + stage
        dst_rel = src_rel - 1 if d == 0 else src_rel + 1
        if stage < 2:
            src, dst = abuf.at[src_rel, m], abuf.at[dst_rel, m]
        else:
            src, dst = abuf.at[src_rel, m, d], abuf.at[dst_rel, m, d]
        return link(src, dst, sf.at[d, lax.rem(m, 2), stage], af.at[d, m, stage], at_z(step, k))

    def push(d, m, stage):
        @pl.when(m >= 2)
        def _():
            forward(d, m - 2, stage).wait_send()

        forward(d, m, stage).start()

    for dlt in range(1, NZ):
        link(pwbuf.at[0], pwbuf.at[NZ - dlt], pws, pwr, at_z(dlt, k)).start()
    for dlt in range(1, NY):
        link(ssbuf.at[0], ssbuf.at[NY - dlt], sss, ssr, at_y(dlt, k)).start()
    for m in range(LEAD):
        for copy in own_copies(m):
            copy.start()
    for child in (0, 1):
        local = pltpu.make_async_copy(panels[child], abuf.at[0, :, k], own_l)
        across = link(panels[child], abuf.at[0, :, k], own_s, own_r, other)

        @pl.when(k == child)
        def _():
            local.start()

        @pl.when(k != child)
        def _():
            across.start()

    all_shifts = link(ssbuf.at[1:NY], ssbuf.at[1:NY], sss, ssr, other)
    all_poles = link(pwbuf.at[1:NZ], pwbuf.at[1:NZ], pws, pwr, other)
    all_shifts.wait_recv()
    block_rows = min(64, kb)

    def basis_block(pos):
        rel = pos + lax.div(pos, 4) - 4 * lax.div(pos, NZ - 1)
        pw = pwbuf[rel]
        pcol[...] = jnp.broadcast_to(pw[0:1, :], (128, kb)).T
        wcol[...] = jnp.broadcast_to(pw[1:2, :], (128, kb)).T
        first = k * child_poles + (y * NZ + lax.rem(z + rel, NZ)) * kb

        @pl.loop(0, NY * (nc // 128))
        def _(tile):
            dest = lax.div(tile, nc // 128)
            lane = pl.multiple_of(lax.rem(tile, nc // 128) * 128, 128)
            shift = ssbuf[dest, 0, :, pl.ds(lane, 128)]
            named = ssbuf[dest, 1, :, pl.ds(lane, 128)]
            kept = named == 2.0 * child_poles
            total = nsend[dest, :, pl.ds(lane, 128)]
            for rb in range(kb // block_rows):
                rows = pl.ds(rb * block_rows, block_rows)
                shape = (block_rows // 8, 8, 128)
                pole = pcol[rows, :].reshape(shape)
                weight = wcol[rows, :].reshape(shape)
                cauchy = weight / (pole - shift[None])
                total = total + jnp.sum(cauchy * cauchy, axis=0)
                ids = (
                    lax.broadcasted_iota(jnp.int32, shape, 0) * 8
                    + lax.broadcasted_iota(jnp.int32, shape, 1)
                    + (first + rb * block_rows)
                ).astype(jnp.float32)
                hot = jnp.where(ids == named[None], 1.0, 0.0)
                value = jnp.where(kept[None], cauchy, hot).reshape(block_rows, 128)
                high = value.astype(jnp.bfloat16)
                low = (value - high.astype(jnp.float32)).astype(jnp.bfloat16)
                at = pl.ds(pl.multiple_of(pos * kb + rb * block_rows, block_rows), block_rows)
                bh[dest, at, pl.ds(lane, 128)] = high
                bl[dest, at, pl.ds(lane, 128)] = low
            nsend[dest, :, pl.ds(lane, 128)] = total

    def send_norms():
        for dlt in range(NY):
            for flip in (0, 1):
                slot = 2 * ((NY - dlt) % NY) + flip
                if slot > 0:
                    core = 1 - k if flip else k
                    link(nsend.at[dlt], nbuf.at[slot], ns, nr, at_y(dlt, core)).start()

    all_norms = link(nbuf.at[1 : 2 * NY], nbuf.at[1 : 2 * NY], ns, nr, other)

    def relay(m, d):
        step = 1 if d == 0 else NY - 1
        return link(
            pbuf.at[2, m, d], rbuf.at[d, m], rls.at[d, lax.rem(m, 2)], rlr.at[d, m], at_y(step, k)
        )

    def final(m, d, o):
        step = 1 if d == 0 else NY - 1
        return link(
            pbuf.at[step, m, o], fbuf.at[m, 2 * k + d], fs.at[d, lax.rem(m, 2), o], fr.at[m],
            at_y(step, o),
        )

    def cross(m):
        return link(pbuf.at[0, m, 1 - k], fbuf.at[m, 4], xs.at[lax.rem(m, 2)], fr.at[m], other)

    def split(rel, m):
        a = abuf[rel, m].reshape(m2, kb)
        high = a.astype(jnp.bfloat16)
        return high, (a - high.astype(jnp.float32)).astype(jnp.bfloat16)

    def split_early(m):
        for pos in range(NZ - 1):
            high, low = split(pos + pos // 4, m)
            ahl[0:m2, pos * kb : (pos + 1) * kb] = high
            ahl[m2 : 2 * m2, pos * kb : (pos + 1) * kb] = low

    early = (NZ - 1) * kb

    def product(a, dest, first, size):
        rows = slice(first, first + size)
        both = jnp.dot(a[...], bh[dest, rows, :], preferred_element_type=jnp.float32)
        rest = jnp.dot(a[0:m2, :], bl[dest, rows, :], preferred_element_type=jnp.float32)
        return (both[0:m2] + (both[m2:] + rest)).reshape(2, half, nc)

    def multiply_early(m, dest):
        pbuf[dest, m] = product(ahl, dest, 0, early)

    def multiply_late(m):
        atail[0:m2, :], atail[m2 : 2 * m2, :] = split(4, m)
        for dest in (2, 1, 3, 0):
            pbuf[dest, m] = pbuf[dest, m] + product(atail, dest, early, kb)
            if dest == 2:
                relay(m, 0).start()
                relay(m, 1).start()
            elif dest == 1:
                final(m, 0, 1).start()
            elif dest == 3:
                final(m, 1, 0).start()
            else:
                cross(m).start()

    def sums_sent(m):
        for d in (0, 1):
            relay(m, d).wait_send()
            final(m, d, 1 - d).wait_send()
        cross(m).wait_send()

    def added_sent(m):
        for d in (0, 1):
            final(m, d, d).wait_send()

    def add_relays(m):
        @pl.when(m >= 2)
        def _():
            added_sent(m - 2)

        relay(m, 0).wait_recv()
        pbuf[1, m, 0] = pbuf[1, m, 0] + rbuf[0, m]
        final(m, 0, 0).start()
        relay(m, 1).wait_recv()
        pbuf[3, m, 1] = pbuf[3, m, 1] + rbuf[1, m]
        final(m, 1, 1).start()

    def finish(m):
        link(fbuf.at[m], fbuf.at[m], xs.at[0], fr.at[m], other).wait_recv()
        factor = scale[0:1, :]
        mine = (pbuf[0, m, k] + (fbuf[m, 2 * k] + fbuf[m, 2 * k + 1])) * factor
        theirs = (fbuf[m, 4] + (fbuf[m, 2 - 2 * k] + fbuf[m, 3 - 2 * k])) * factor
        out[k, m] = mine
        out[1 - k, m] = theirs
        squares = (mine * mine + theirs * theirs).reshape(half // 8, 8, nc)
        sq[...] = sq[...] + jnp.sum(squares, axis=0)

    def within(m):
        return jnp.logical_and(m >= 0, m < nm)

    @pl.loop(0, nm + 7)
    def _(t):
        @pl.when(t < 3)
        def _():
            basis_block(3 * t)

        @pl.when(t == 0)
        def _():
            all_poles.wait_recv()

        @pl.when(within(t))
        def _():
            for d in (0, 1):
                first_wait(d, t).wait_recv()
                push(d, t, 0)

        @pl.when(within(t - 4))
        def _():
            for d in (0, 1):
                forward(d, t - 4, 2).wait_recv()

            @pl.when(t >= 6)
            def _():
                sums_sent(t - 6)

            multiply_late(t - 4)

        @pl.when(t == 3)
        def _():
            pltpu.make_async_copy(up, abuf.at[0, :, k], own_l).wait()
            link(up, abuf.at[0, :, 1 - k], own_s, own_r, other).wait_recv()
            send_norms()
            nbuf[0] = nsend[0]

        @pl.when(within(t - 3))
        def _():
            split_early(t - 3)
            multiply_early(t - 3, 2)

        @pl.when(within(t - 5))
        def _():
            add_relays(t - 5)

        @pl.when(t < 3)
        def _():
            basis_block(3 * t + 1)

        @pl.when(within(t - 3))
        def _():
            multiply_early(t - 3, 1)

        @pl.when(within(t - 3))
        def _():
            multiply_early(t - 3, 3)

        @pl.when(within(t - 1))
        def _():
            for d in (0, 1):
                forward(d, t - 1, 0).wait_recv()
                push(d, t - 1, 1)

        @pl.when(t < 2)
        def _():
            basis_block(3 * t + 2)

        @pl.when(within(t - 3))
        def _():
            multiply_early(t - 3, 0)

        @pl.when(within(t - 2))
        def _():
            for d in (0, 1):
                forward(d, t - 2, 1).wait_recv()
                push(d, t - 2, 2)

        @pl.when(t + 3 < nm)
        def _():
            @pl.when(t + 3 >= 4)
            def _():
                for copy in own_copies(t - 1):
                    copy.wait_send()

            for copy in own_copies(t + 3):
                copy.start()

        @pl.when(t == 7)
        def _():
            all_norms.wait_recv()
            total = nbuf[0]
            for slot in range(1, 2 * NY):
                total = total + nbuf[slot]
            sums = jnp.sum(total, axis=0, keepdims=True)
            kept = ssbuf[0, 1, 0:1, :] == 2.0 * child_poles
            scale[...] = jnp.broadcast_to(
                jnp.where(kept, 1.0 / jnp.sqrt(sums), 1.0), (8, nc)
            )

        @pl.when(within(t - 7))
        def _():
            finish(t - 7)

    wbuf[0] = jnp.sum(sq[...], axis=0, keepdims=True)
    for dlt in range(1, n_row):
        link(wbuf.at[0], wbuf.at[n_row - dlt], ws, wr, at_row(dlt)).start()
    all_weights = link(wbuf.at[1:n_row], wbuf.at[1:n_row], ws, wr, other)

    all_poles.wait_send()
    all_shifts.wait_send()
    link(up, abuf.at[0, :, k], own_s, own_r, other).wait_send()
    all_norms.wait_send()

    for m in range(nm - 4, nm):
        for copy in own_copies(m):
            copy.wait_send()
    for m in range(nm - 2, nm):
        for d in (0, 1):
            for stage in (0, 1, 2):
                forward(d, m, stage).wait_send()
        sums_sent(m)
        added_sent(m)

    weight_sum = wbuf[0]
    all_weights.wait_recv()
    for dlt in range(1, n_row):
        weight_sum = weight_sum + wbuf[dlt]
    rows_all = 2 * n_row * nm * half
    slab[...] = weight_sum * (1.0 / rows_all)
    all_weights.wait_send()


def local(n_row, upper_panel, lower_panel, pole_values, coupling, kept_mask, shifts, source):
    rows, kb = upper_panel.shape
    nc = shifts.shape[0]
    nm = CHUNKS
    half = rows // nm
    m2 = 2 * half
    child_poles = NZ * NY * kb
    kpart = NZ * kb
    f32 = jnp.float32
    dma = pltpu.SemaphoreType.DMA
    vmem = pl.BlockSpec(memory_space=pltpu.VMEM)
    hbm = pl.BlockSpec(memory_space=pltpu.HBM)
    out, slab = pl.pallas_call(
        functools.partial(kernel, n_row, child_poles),
        out_shape=(
            jax.ShapeDtypeStruct((2, nm, half, nc), f32),
            jax.ShapeDtypeStruct((1, nc), f32),
        ),
        in_specs=[hbm] * 7,
        out_specs=(vmem, vmem),
        scratch_shapes=[
            pltpu.VMEM((NZ, nm, 2, half, kb), f32),
            pltpu.VMEM((2 * m2, kpart - kb), jnp.bfloat16),
            pltpu.VMEM((2 * m2, kb), jnp.bfloat16),
            pltpu.VMEM((NY, kpart, nc), jnp.bfloat16),
            pltpu.VMEM((NY, kpart, nc), jnp.bfloat16),
            pltpu.VMEM((NY, nm, 2, half, nc), f32),
            pltpu.VMEM((2, nm, half, nc), f32),
            pltpu.VMEM((nm, 5, half, nc), f32),
            pltpu.VMEM((NZ, 8, kb), f32),
            pltpu.VMEM((NY, 2, 8, nc), f32),
            pltpu.VMEM((NY, 8, nc), f32),
            pltpu.VMEM((2 * NY, 8, nc), f32),
            pltpu.VMEM((kb, 128), f32),
            pltpu.VMEM((kb, 128), f32),
            pltpu.VMEM((8, nc), f32),
            pltpu.VMEM((8, nc), f32),
            pltpu.VMEM((n_row, 1, nc), f32),
            pltpu.VMEM((2, kb), f32),
            pltpu.VMEM((2, kb), f32),
            pltpu.VMEM((2, kb), jnp.int32),
            pltpu.VMEM((1, nc), f32),
            pltpu.VMEM((1, nc), jnp.int32),
            dma, dma, dma,
            dma((2, 4, 2)), dma((2, nm)),
            dma((2, 2, 3)), dma((2, nm, 3)),
            dma, dma, dma, dma, dma, dma,
            dma((2, 2)), dma((2, nm)),
            dma((2, 2, 2)), dma((nm,)),
            dma((2,)), dma, dma, dma((5,)),
        ],
        compiler_params=pltpu.CompilerParams(
            collective_id=0, has_side_effects=True, vmem_limit_bytes=50 * 1024 * 1024
        ),
    )(
        *(
            pltpu.with_memory_space_constraint(given, pltpu.HBM)
            for given in (
                upper_panel.reshape(nm, half, kb),
                lower_panel.reshape(nm, half, kb),
                pole_values,
                coupling,
                kept_mask,
                shifts.reshape(1, nc),
                source.reshape(1, nc),
            )
        )
    )
    return out.reshape(2, rows, nc), slab.reshape(nc)


def solution(mesh):
    in_specs = (
        P("row", "col"),
        P("row", "col"),
        P(None, "col"),
        P(None, "col"),
        P(None, "col"),
        P("col"),
        P("col"),
    )
    out_specs = (P(None, "row", "col"), P("col"))
    body = functools.partial(local, mesh.shape["row"])
    return jax.shard_map(body, mesh=mesh, in_specs=in_specs, out_specs=out_specs, check_vma=False)
```

```python
import functools

import jax
import jax.numpy as jnp
from jax import lax
from jax.experimental import pallas as pl
from jax.experimental.pallas import tpu as pltpu
from jax.sharding import PartitionSpec as P

NZ = 8
NY = 4
CHUNKS = 8
LEAD = 3
MESH = pl.DeviceIdType.MESH


def link(src, dst, ssem, rsem, dev):
    return pltpu.make_async_remote_copy(
        src_ref=src, dst_ref=dst, send_sem=ssem, recv_sem=rsem, device_id=dev, device_id_type=MESH
    )


def kernel(
    n_row, child_poles,
    up, lo, poles_in, coup_in, mask_in, shifts_in, source_in,
    out, slab,
    abuf, ahl, atail, bh, bl, pbuf, rbuf, fbuf,
    pwbuf, ssbuf, nsend, nbuf, pcol, wcol, scale, sq, wbuf,
    poles, coup, mask, shifts, source,
    own_l, own_s, own_r, s1, a1, sf, af, pws, pwr, sss, ssr, ns, nr,
    rls, rlr, fs, fr, xs, ws, wr, isem,
):
    r = lax.axis_index("row")
    c = lax.axis_index("col")
    k = lax.rem(r, 2)
    r0 = r - k
    y = lax.div(c, NZ)
    z = lax.rem(c, NZ)
    nm = CHUNKS
    half = up.shape[1]
    kb = up.shape[2]
    m2 = 2 * half
    nc = shifts.shape[1]
    fetches = [
        pltpu.make_async_copy(given, held, isem.at[n])
        for n, (given, held) in enumerate(
            zip(
                (poles_in, coup_in, mask_in, shifts_in, source_in),
                (poles, coup, mask, shifts, source),
            )
        )
    ]
    for fetch in fetches:
        fetch.start()

    def at_z(delta, core):
        return (r0 + core, y * NZ + lax.rem(z + delta + NZ, NZ))

    def at_y(delta, core):
        return (r0 + core, lax.rem(y + delta + NY, NY) * NZ + z)

    def at_row(delta):
        return (lax.rem(r + delta, n_row), c)

    other = (r0 + 1 - k, c)

    barrier = pltpu.get_barrier_semaphore()
    peers = [at_z(d, k) for d in range(1, NZ)] + [at_z(1, 1 - k), at_z(NZ - 1, 1 - k)]
    peers += [at_y(d, q) for d in range(1, NY) for q in (0, 1)]
    peers += [at_row(d) for d in range(1, n_row)]
    for dev in peers:
        pl.semaphore_signal(barrier, inc=1, device_id=dev, device_id_type=MESH)

    for fetch in fetches:
        fetch.wait()
    pw_rows = lax.broadcasted_iota(jnp.int32, (8, kb), 0)
    pole_row = jnp.broadcast_to(poles[pl.ds(k, 1), :], (8, kb))
    weight_row = jnp.broadcast_to(
        coup[pl.ds(k, 1), :] * mask[pl.ds(k, 1), :].astype(jnp.float32), (8, kb)
    )
    pwbuf[0] = jnp.where(pw_rows == 0, pole_row, weight_row)
    ssbuf[0, 0] = jnp.broadcast_to(shifts[...], (8, nc))
    ssbuf[0, 1] = jnp.broadcast_to(source[...].astype(jnp.float32), (8, nc))
    nsend[...] = jnp.zeros_like(nsend)
    sq[...] = jnp.zeros_like(sq)

    pl.semaphore_wait(barrier, len(peers))

    panels = (up, lo)

    def own_copies(m):
        return [
            link(
                panels[child].at[m], abuf.at[NZ - 1 if step == 1 else 1, m, k],
                s1.at[d, lax.rem(m, 4), child], a1.at[d, m], at_z(step, child),
            )
            for d, step in ((0, 1), (1, NZ - 1))
            for child in (0, 1)
        ]

    def first_wait(d, m):
        dst = abuf.at[NZ - 1 if d == 0 else 1, m]
        return link(dst, dst, s1.at[d, 0, 0], a1.at[d, m], other)

    def forward(d, m, stage):
        step = 1 if d == 0 else NZ - 1
        src_rel = NZ - 1 - stage if d == 0 else 1 + stage
        dst_rel = src_rel - 1 if d == 0 else src_rel + 1
        if stage < 2:
            src, dst = abuf.at[src_rel, m], abuf.at[dst_rel, m]
        else:
            src, dst = abuf.at[src_rel, m, d], abuf.at[dst_rel, m, d]
        return link(src, dst, sf.at[d, lax.rem(m, 2), stage], af.at[d, m, stage], at_z(step, k))

    def push(d, m, stage):
        @pl.when(m >= 2)
        def _():
            forward(d, m - 2, stage).wait_send()

        forward(d, m, stage).start()

    for dlt in range(1, NZ):
        link(pwbuf.at[0], pwbuf.at[NZ - dlt], pws, pwr, at_z(dlt, k)).start()
    for dlt in range(1, NY):
        link(ssbuf.at[0], ssbuf.at[NY - dlt], sss, ssr, at_y(dlt, k)).start()
    for m in range(LEAD):
        for copy in own_copies(m):
            copy.start()
    for child in (0, 1):
        local = pltpu.make_async_copy(panels[child], abuf.at[0, :, k], own_l)
        across = link(panels[child], abuf.at[0, :, k], own_s, own_r, other)

        @pl.when(k == child)
        def _():
            local.start()

        @pl.when(k != child)
        def _():
            across.start()

    all_shifts = link(ssbuf.at[1:NY], ssbuf.at[1:NY], sss, ssr, other)
    all_poles = link(pwbuf.at[1:NZ], pwbuf.at[1:NZ], pws, pwr, other)
    all_shifts.wait_recv()
    block_rows = min(64, kb)

    def basis_block(pos):
        rel = pos + lax.div(pos, 4) - 4 * lax.div(pos, NZ - 1)
        pw = pwbuf[rel]
        pcol[...] = jnp.broadcast_to(pw[0:1, :], (128, kb)).T
        wcol[...] = jnp.broadcast_to(pw[1:2, :], (128, kb)).T
        first = k * child_poles + (y * NZ + lax.rem(z + rel, NZ)) * kb

        tall = (block_rows // 8, 8, 128)
        ids = (
            lax.broadcasted_iota(jnp.int32, tall, 0) * 8 + lax.broadcasted_iota(jnp.int32, tall, 1)
        ).astype(jnp.float32)

        @pl.loop(0, NY * (nc // 128))
        def _(tile):
            dest = lax.div(tile, nc // 128)
            lane = pl.multiple_of(lax.rem(tile, nc // 128) * 128, 128)
            shift = ssbuf[dest, 0, :, pl.ds(lane, 128)]
            named = ssbuf[dest, 1, :, pl.ds(lane, 128)]
            kept = named == 2.0 * child_poles
            total = nsend[dest, :, pl.ds(lane, 128)]
            for rb in range(kb // block_rows):
                rows = pl.ds(rb * block_rows, block_rows)
                shape = (block_rows // 8, 8, 128)
                pole = pcol[rows, :].reshape(shape)
                weight = wcol[rows, :].reshape(shape)
                cauchy = weight / (pole - shift[None])
                total = total + jnp.sum(cauchy * cauchy, axis=0)
                at_row_here = named - (first + rb * block_rows).astype(jnp.float32)
                hot = jnp.where(ids == at_row_here[None], 1.0, 0.0)
                value = jnp.where(kept[None], cauchy, hot).reshape(block_rows, 128)
                high = value.astype(jnp.bfloat16)
                low = (value - high.astype(jnp.float32)).astype(jnp.bfloat16)
                at = pl.ds(pl.multiple_of(pos * kb + rb * block_rows, block_rows), block_rows)
                bh[dest, at, pl.ds(lane, 128)] = high
                bl[dest, at, pl.ds(lane, 128)] = low
            nsend[dest, :, pl.ds(lane, 128)] = total

    def send_norms():
        for dlt in range(NY):
            for flip in (0, 1):
                slot = 2 * ((NY - dlt) % NY) + flip
                if slot > 0:
                    core = 1 - k if flip else k
                    link(nsend.at[dlt], nbuf.at[slot], ns, nr, at_y(dlt, core)).start()

    all_norms = link(nbuf.at[1 : 2 * NY], nbuf.at[1 : 2 * NY], ns, nr, other)

    def relay(m, d):
        step = 1 if d == 0 else NY - 1
        return link(
            pbuf.at[2, m, d], rbuf.at[d, m], rls.at[d, lax.rem(m, 2)], rlr.at[d, m], at_y(step, k)
        )

    def final(m, d, o):
        step = 1 if d == 0 else NY - 1
        return link(
            pbuf.at[step, m, o], fbuf.at[m, 2 * k + d], fs.at[d, lax.rem(m, 2), o], fr.at[m],
            at_y(step, o),
        )

    def cross(m):
        return link(pbuf.at[0, m, 1 - k], fbuf.at[m, 4], xs.at[lax.rem(m, 2)], fr.at[m], other)

    def split(rel, m):
        a = abuf[rel, m].reshape(m2, kb)
        high = a.astype(jnp.bfloat16)
        return high, (a - high.astype(jnp.float32)).astype(jnp.bfloat16)

    def split_early(m):
        for pos in range(NZ - 1):
            high, low = split(pos + pos // 4, m)
            ahl[0:m2, pos * kb : (pos + 1) * kb] = high
            ahl[m2 : 2 * m2, pos * kb : (pos + 1) * kb] = low

    early = (NZ - 1) * kb

    def product(a, dest, first, size):
        rows = slice(first, first + size)
        both = jnp.dot(a[...], bh[dest, rows, :], preferred_element_type=jnp.float32)
        rest = jnp.dot(a[0:m2, :], bl[dest, rows, :], preferred_element_type=jnp.float32)
        return (both[0:m2] + (both[m2:] + rest)).reshape(2, half, nc)

    def multiply_early(m, dest):
        pbuf[dest, m] = product(ahl, dest, 0, early)

    def multiply_late(m):
        atail[0:m2, :], atail[m2 : 2 * m2, :] = split(4, m)
        for dest in (2, 1, 3, 0):
            pbuf[dest, m] = pbuf[dest, m] + product(atail, dest, early, kb)
            if dest == 2:
                relay(m, 0).start()
                relay(m, 1).start()
            elif dest == 1:
                final(m, 0, 1).start()
            elif dest == 3:
                final(m, 1, 0).start()
            else:
                cross(m).start()

    def sums_sent(m):
        for d in (0, 1):
            relay(m, d).wait_send()
            final(m, d, 1 - d).wait_send()
        cross(m).wait_send()

    def added_sent(m):
        for d in (0, 1):
            final(m, d, d).wait_send()

    def add_relays(m):
        @pl.when(m >= 2)
        def _():
            added_sent(m - 2)

        relay(m, 0).wait_recv()
        pbuf[1, m, 0] = pbuf[1, m, 0] + rbuf[0, m]
        final(m, 0, 0).start()
        relay(m, 1).wait_recv()
        pbuf[3, m, 1] = pbuf[3, m, 1] + rbuf[1, m]
        final(m, 1, 1).start()

    def finish(m):
        link(fbuf.at[m], fbuf.at[m], xs.at[0], fr.at[m], other).wait_recv()
        factor = scale[0:1, :]
        mine = (pbuf[0, m, k] + (fbuf[m, 2 * k] + fbuf[m, 2 * k + 1])) * factor
        theirs = (fbuf[m, 4] + (fbuf[m, 2 - 2 * k] + fbuf[m, 3 - 2 * k])) * factor
        out[k, m] = mine
        out[1 - k, m] = theirs
        squares = (mine * mine + theirs * theirs).reshape(half // 8, 8, nc)
        sq[...] = sq[...] + jnp.sum(squares, axis=0)

    def within(m):
        return jnp.logical_and(m >= 0, m < nm)

    @pl.loop(0, nm + 7)
    def _(t):
        @pl.when(t < 3)
        def _():
            basis_block(3 * t)

        @pl.when(t == 0)
        def _():
            all_poles.wait_recv()

        @pl.when(within(t))
        def _():
            for d in (0, 1):
                first_wait(d, t).wait_recv()
                push(d, t, 0)

        @pl.when(within(t - 4))
        def _():
            for d in (0, 1):
                forward(d, t - 4, 2).wait_recv()

            @pl.when(t >= 6)
            def _():
                sums_sent(t - 6)

            multiply_late(t - 4)

        @pl.when(t == 3)
        def _():
            pltpu.make_async_copy(up, abuf.at[0, :, k], own_l).wait()
            link(up, abuf.at[0, :, 1 - k], own_s, own_r, other).wait_recv()
            send_norms()
            nbuf[0] = nsend[0]

        @pl.when(within(t - 3))
        def _():
            split_early(t - 3)
            multiply_early(t - 3, 2)

        @pl.when(within(t - 5))
        def _():
            add_relays(t - 5)

        @pl.when(t < 3)
        def _():
            basis_block(3 * t + 1)

        @pl.when(within(t - 3))
        def _():
            multiply_early(t - 3, 1)

        @pl.when(within(t - 3))
        def _():
            multiply_early(t - 3, 3)

        @pl.when(within(t - 1))
        def _():
            for d in (0, 1):
                forward(d, t - 1, 0).wait_recv()
                push(d, t - 1, 1)

        @pl.when(t < 2)
        def _():
            basis_block(3 * t + 2)

        @pl.when(within(t - 3))
        def _():
            multiply_early(t - 3, 0)

        @pl.when(within(t - 2))
        def _():
            for d in (0, 1):
                forward(d, t - 2, 1).wait_recv()
                push(d, t - 2, 2)

        @pl.when(t + 3 < nm)
        def _():
            @pl.when(t + 3 >= 4)
            def _():
                for copy in own_copies(t - 1):
                    copy.wait_send()

            for copy in own_copies(t + 3):
                copy.start()

        @pl.when(t == 7)
        def _():
            all_norms.wait_recv()
            total = nbuf[0]
            for slot in range(1, 2 * NY):
                total = total + nbuf[slot]
            sums = jnp.sum(total, axis=0, keepdims=True)
            kept = ssbuf[0, 1, 0:1, :] == 2.0 * child_poles
            scale[...] = jnp.broadcast_to(
                jnp.where(kept, 1.0 / jnp.sqrt(sums), 1.0), (8, nc)
            )

        @pl.when(within(t - 7))
        def _():
            finish(t - 7)

    wbuf[0] = jnp.sum(sq[...], axis=0, keepdims=True)
    for dlt in range(1, n_row):
        link(wbuf.at[0], wbuf.at[n_row - dlt], ws, wr, at_row(dlt)).start()
    all_weights = link(wbuf.at[1:n_row], wbuf.at[1:n_row], ws, wr, other)

    all_poles.wait_send()
    all_shifts.wait_send()
    link(up, abuf.at[0, :, k], own_s, own_r, other).wait_send()
    all_norms.wait_send()

    for m in range(nm - 4, nm):
        for copy in own_copies(m):
            copy.wait_send()
    for m in range(nm - 2, nm):
        for d in (0, 1):
            for stage in (0, 1, 2):
                forward(d, m, stage).wait_send()
        sums_sent(m)
        added_sent(m)

    weight_sum = wbuf[0]
    all_weights.wait_recv()
    for dlt in range(1, n_row):
        weight_sum = weight_sum + wbuf[dlt]
    rows_all = 2 * n_row * nm * half
    slab[...] = weight_sum * (1.0 / rows_all)
    all_weights.wait_send()


def local(n_row, upper_panel, lower_panel, pole_values, coupling, kept_mask, shifts, source):
    rows, kb = upper_panel.shape
    nc = shifts.shape[0]
    nm = CHUNKS
    half = rows // nm
    m2 = 2 * half
    child_poles = NZ * NY * kb
    kpart = NZ * kb
    f32 = jnp.float32
    dma = pltpu.SemaphoreType.DMA
    vmem = pl.BlockSpec(memory_space=pltpu.VMEM)
    hbm = pl.BlockSpec(memory_space=pltpu.HBM)
    out, slab = pl.pallas_call(
        functools.partial(kernel, n_row, child_poles),
        out_shape=(
            jax.ShapeDtypeStruct((2, nm, half, nc), f32),
            jax.ShapeDtypeStruct((1, nc), f32),
        ),
        in_specs=[hbm] * 7,
        out_specs=(vmem, vmem),
        scratch_shapes=[
            pltpu.VMEM((NZ, nm, 2, half, kb), f32),
            pltpu.VMEM((2 * m2, kpart - kb), jnp.bfloat16),
            pltpu.VMEM((2 * m2, kb), jnp.bfloat16),
            pltpu.VMEM((NY, kpart, nc), jnp.bfloat16),
            pltpu.VMEM((NY, kpart, nc), jnp.bfloat16),
            pltpu.VMEM((NY, nm, 2, half, nc), f32),
            pltpu.VMEM((2, nm, half, nc), f32),
            pltpu.VMEM((nm, 5, half, nc), f32),
            pltpu.VMEM((NZ, 8, kb), f32),
            pltpu.VMEM((NY, 2, 8, nc), f32),
            pltpu.VMEM((NY, 8, nc), f32),
            pltpu.VMEM((2 * NY, 8, nc), f32),
            pltpu.VMEM((kb, 128), f32),
            pltpu.VMEM((kb, 128), f32),
            pltpu.VMEM((8, nc), f32),
            pltpu.VMEM((8, nc), f32),
            pltpu.VMEM((n_row, 1, nc), f32),
            pltpu.VMEM((2, kb), f32),
            pltpu.VMEM((2, kb), f32),
            pltpu.VMEM((2, kb), jnp.int32),
            pltpu.VMEM((1, nc), f32),
            pltpu.VMEM((1, nc), jnp.int32),
            dma, dma, dma,
            dma((2, 4, 2)), dma((2, nm)),
            dma((2, 2, 3)), dma((2, nm, 3)),
            dma, dma, dma, dma, dma, dma,
            dma((2, 2)), dma((2, nm)),
            dma((2, 2, 2)), dma((nm,)),
            dma((2,)), dma, dma, dma((5,)),
        ],
        compiler_params=pltpu.CompilerParams(
            collective_id=0, has_side_effects=True, vmem_limit_bytes=50 * 1024 * 1024
        ),
    )(
        *(
            pltpu.with_memory_space_constraint(given, pltpu.HBM)
            for given in (
                upper_panel.reshape(nm, half, kb),
                lower_panel.reshape(nm, half, kb),
                pole_values,
                coupling,
                kept_mask,
                shifts.reshape(1, nc),
                source.reshape(1, nc),
            )
        )
    )
    return out.reshape(2, rows, nc), slab.reshape(nc)


def solution(mesh):
    in_specs = (
        P("row", "col"),
        P("row", "col"),
        P(None, "col"),
        P(None, "col"),
        P(None, "col"),
        P("col"),
        P("col"),
    )
    out_specs = (P(None, "row", "col"), P("col"))
    body = functools.partial(local, mesh.shape["row"])
    return jax.shard_map(body, mesh=mesh, in_specs=in_specs, out_specs=out_specs, check_vma=False)
```

```python
import functools

import jax
import jax.numpy as jnp
from jax import lax
from jax.experimental import pallas as pl
from jax.experimental.pallas import tpu as pltpu
from jax.sharding import PartitionSpec as P

NZ = 8
NY = 4
CHUNKS = 8
LEAD = 4
MESH = pl.DeviceIdType.MESH


def link(src, dst, ssem, rsem, dev):
    return pltpu.make_async_remote_copy(
        src_ref=src, dst_ref=dst, send_sem=ssem, recv_sem=rsem, device_id=dev, device_id_type=MESH
    )


def kernel(
    n_row, child_poles,
    up, lo, poles_in, coup_in, mask_in, shifts_in, source_in,
    out, slab,
    abuf, ahl, atail, bh, bl, pbuf, rbuf, fbuf,
    pwbuf, ssbuf, nsend, nbuf, pcol, wcol, scale, sq, wbuf,
    poles, coup, mask, shifts, source,
    own_l, own_s, own_r, s1, a1, sf, af, pws, pwr, sss, ssr, ns, nr,
    rls, rlr, fs, fr, xs, ws, wr, isem,
):
    r = lax.axis_index("row")
    c = lax.axis_index("col")
    k = lax.rem(r, 2)
    r0 = r - k
    y = lax.div(c, NZ)
    z = lax.rem(c, NZ)
    nm = CHUNKS
    half = up.shape[1]
    kb = up.shape[2]
    m2 = 2 * half
    nc = shifts.shape[1]
    fetches = [
        pltpu.make_async_copy(given, held, isem.at[n])
        for n, (given, held) in enumerate(
            zip(
                (poles_in, coup_in, mask_in, shifts_in, source_in),
                (poles, coup, mask, shifts, source),
            )
        )
    ]
    for fetch in fetches:
        fetch.start()

    def at_z(delta, core):
        return (r0 + core, y * NZ + lax.rem(z + delta + NZ, NZ))

    def at_y(delta, core):
        return (r0 + core, lax.rem(y + delta + NY, NY) * NZ + z)

    def at_row(delta):
        return (lax.rem(r + delta, n_row), c)

    other = (r0 + 1 - k, c)

    barrier = pltpu.get_barrier_semaphore()
    peers = [at_z(d, k) for d in range(1, NZ)] + [at_z(1, 1 - k), at_z(NZ - 1, 1 - k)]
    peers += [at_y(d, q) for d in range(1, NY) for q in (0, 1)]
    peers += [at_row(d) for d in range(1, n_row)]
    for dev in peers:
        pl.semaphore_signal(barrier, inc=1, device_id=dev, device_id_type=MESH)

    for fetch in fetches:
        fetch.wait()
    pw_rows = lax.broadcasted_iota(jnp.int32, (8, kb), 0)
    pole_row = jnp.broadcast_to(poles[pl.ds(k, 1), :], (8, kb))
    weight_row = jnp.broadcast_to(
        coup[pl.ds(k, 1), :] * mask[pl.ds(k, 1), :].astype(jnp.float32), (8, kb)
    )
    pwbuf[0] = jnp.where(pw_rows == 0, pole_row, weight_row)
    ssbuf[0, 0] = jnp.broadcast_to(shifts[...], (8, nc))
    ssbuf[0, 1] = jnp.broadcast_to(source[...].astype(jnp.float32), (8, nc))
    nsend[...] = jnp.zeros_like(nsend)
    sq[...] = jnp.zeros_like(sq)

    pl.semaphore_wait(barrier, len(peers))

    panels = (up, lo)

    def own_copies(m):
        return [
            link(
                panels[child].at[m], abuf.at[NZ - 1 if step == 1 else 1, m, k],
                s1.at[d, lax.rem(m, 4), child], a1.at[d, m], at_z(step, child),
            )
            for d, step in ((0, 1), (1, NZ - 1))
            for child in (0, 1)
        ]

    def first_wait(d, m):
        dst = abuf.at[NZ - 1 if d == 0 else 1, m]
        return link(dst, dst, s1.at[d, 0, 0], a1.at[d, m], other)

    def forward(d, m, stage):
        step = 1 if d == 0 else NZ - 1
        src_rel = NZ - 1 - stage if d == 0 else 1 + stage
        dst_rel = src_rel - 1 if d == 0 else src_rel + 1
        if stage < 2:
            src, dst = abuf.at[src_rel, m], abuf.at[dst_rel, m]
        else:
            src, dst = abuf.at[src_rel, m, d], abuf.at[dst_rel, m, d]
        return link(src, dst, sf.at[d, lax.rem(m, 2), stage], af.at[d, m, stage], at_z(step, k))

    def push(d, m, stage):
        @pl.when(m >= 2)
        def _():
            forward(d, m - 2, stage).wait_send()

        forward(d, m, stage).start()

    for dlt in range(1, NZ):
        link(pwbuf.at[0], pwbuf.at[NZ - dlt], pws, pwr, at_z(dlt, k)).start()
    for dlt in range(1, NY):
        link(ssbuf.at[0], ssbuf.at[NY - dlt], sss, ssr, at_y(dlt, k)).start()
    for m in range(LEAD):
        for copy in own_copies(m):
            copy.start()
    for child in (0, 1):
        local = pltpu.make_async_copy(panels[child], abuf.at[0, :, k], own_l)
        across = link(panels[child], abuf.at[0, :, k], own_s, own_r, other)

        @pl.when(k == child)
        def _():
            local.start()

        @pl.when(k != child)
        def _():
            across.start()

    all_shifts = link(ssbuf.at[1:NY], ssbuf.at[1:NY], sss, ssr, other)
    all_poles = link(pwbuf.at[1:NZ], pwbuf.at[1:NZ], pws, pwr, other)
    all_shifts.wait_recv()
    block_rows = min(64, kb)

    def basis_block(pos):
        rel = pos + lax.div(pos, 4) - 4 * lax.div(pos, NZ - 1)
        pw = pwbuf[rel]
        pcol[...] = jnp.broadcast_to(pw[0:1, :], (128, kb)).T
        wcol[...] = jnp.broadcast_to(pw[1:2, :], (128, kb)).T
        first = k * child_poles + (y * NZ + lax.rem(z + rel, NZ)) * kb

        tall = (block_rows // 8, 8, 128)
        ids = (
            lax.broadcasted_iota(jnp.int32, tall, 0) * 8 + lax.broadcasted_iota(jnp.int32, tall, 1)
        ).astype(jnp.float32)

        @pl.loop(0, NY * (nc // 128))
        def _(tile):
            dest = lax.div(tile, nc // 128)
            lane = pl.multiple_of(lax.rem(tile, nc // 128) * 128, 128)
            shift = ssbuf[dest, 0, :, pl.ds(lane, 128)]
            named = ssbuf[dest, 1, :, pl.ds(lane, 128)]
            kept = named == 2.0 * child_poles
            total = nsend[dest, :, pl.ds(lane, 128)]
            for rb in range(kb // block_rows):
                rows = pl.ds(rb * block_rows, block_rows)
                shape = (block_rows // 8, 8, 128)
                pole = pcol[rows, :].reshape(shape)
                weight = wcol[rows, :].reshape(shape)
                cauchy = weight / (pole - shift[None])
                total = total + jnp.sum(cauchy * cauchy, axis=0)
                at_row_here = named - (first + rb * block_rows).astype(jnp.float32)
                hot = jnp.where(ids == at_row_here[None], 1.0, 0.0)
                value = jnp.where(kept[None], cauchy, hot).reshape(block_rows, 128)
                high = value.astype(jnp.bfloat16)
                low = (value - high.astype(jnp.float32)).astype(jnp.bfloat16)
                at = pl.ds(pl.multiple_of(pos * kb + rb * block_rows, block_rows), block_rows)
                bh[dest, at, pl.ds(lane, 128)] = high
                bl[dest, at, pl.ds(lane, 128)] = low
            nsend[dest, :, pl.ds(lane, 128)] = total

    def send_norms():
        for dlt in range(NY):
            for flip in (0, 1):
                slot = 2 * ((NY - dlt) % NY) + flip
                if slot > 0:
                    core = 1 - k if flip else k
                    link(nsend.at[dlt], nbuf.at[slot], ns, nr, at_y(dlt, core)).start()

    all_norms = link(nbuf.at[1 : 2 * NY], nbuf.at[1 : 2 * NY], ns, nr, other)

    def relay(m, d):
        step = 1 if d == 0 else NY - 1
        return link(
            pbuf.at[2, m, d], rbuf.at[d, m], rls.at[d, lax.rem(m, 2)], rlr.at[d, m], at_y(step, k)
        )

    def final(m, d, o):
        step = 1 if d == 0 else NY - 1
        return link(
            pbuf.at[step, m, o], fbuf.at[m, 2 * k + d], fs.at[d, lax.rem(m, 2), o], fr.at[m],
            at_y(step, o),
        )

    def cross(m):
        return link(pbuf.at[0, m, 1 - k], fbuf.at[m, 4], xs.at[lax.rem(m, 2)], fr.at[m], other)

    def split(rel, m):
        a = abuf[rel, m].reshape(m2, kb)
        high = a.astype(jnp.bfloat16)
        return high, (a - high.astype(jnp.float32)).astype(jnp.bfloat16)

    def split_early(m):
        for pos in range(NZ - 1):
            high, low = split(pos + pos // 4, m)
            ahl[0:m2, pos * kb : (pos + 1) * kb] = high
            ahl[m2 : 2 * m2, pos * kb : (pos + 1) * kb] = low

    early = (NZ - 1) * kb

    def product(a, dest, first, size):
        rows = slice(first, first + size)
        both = jnp.dot(a[...], bh[dest, rows, :], preferred_element_type=jnp.float32)
        rest = jnp.dot(a[0:m2, :], bl[dest, rows, :], preferred_element_type=jnp.float32)
        return (both[0:m2] + (both[m2:] + rest)).reshape(2, half, nc)

    def multiply_early(m, dest):
        pbuf[dest, m] = product(ahl, dest, 0, early)

    def multiply_late(m):
        atail[0:m2, :], atail[m2 : 2 * m2, :] = split(4, m)
        for dest in (2, 1, 3, 0):
            pbuf[dest, m] = pbuf[dest, m] + product(atail, dest, early, kb)
            if dest == 2:
                relay(m, 0).start()
                relay(m, 1).start()
            elif dest == 1:
                final(m, 0, 1).start()
            elif dest == 3:
                final(m, 1, 0).start()
            else:
                cross(m).start()

    def sums_sent(m):
        for d in (0, 1):
            relay(m, d).wait_send()
            final(m, d, 1 - d).wait_send()
        cross(m).wait_send()

    def added_sent(m):
        for d in (0, 1):
            final(m, d, d).wait_send()

    def add_relays(m):
        @pl.when(m >= 2)
        def _():
            added_sent(m - 2)

        relay(m, 0).wait_recv()
        pbuf[1, m, 0] = pbuf[1, m, 0] + rbuf[0, m]
        final(m, 0, 0).start()
        relay(m, 1).wait_recv()
        pbuf[3, m, 1] = pbuf[3, m, 1] + rbuf[1, m]
        final(m, 1, 1).start()

    def finish(m):
        link(fbuf.at[m], fbuf.at[m], xs.at[0], fr.at[m], other).wait_recv()
        factor = scale[0:1, :]
        mine = (pbuf[0, m, k] + (fbuf[m, 2 * k] + fbuf[m, 2 * k + 1])) * factor
        theirs = (fbuf[m, 4] + (fbuf[m, 2 - 2 * k] + fbuf[m, 3 - 2 * k])) * factor
        out[k, m] = mine
        out[1 - k, m] = theirs
        squares = (mine * mine + theirs * theirs).reshape(half // 8, 8, nc)
        sq[...] = sq[...] + jnp.sum(squares, axis=0)

    def within(m):
        return jnp.logical_and(m >= 0, m < nm)

    @pl.loop(0, nm + 7)
    def _(t):
        @pl.when(t < 3)
        def _():
            basis_block(3 * t)

        @pl.when(t == 0)
        def _():
            all_poles.wait_recv()

        @pl.when(within(t))
        def _():
            for d in (0, 1):
                first_wait(d, t).wait_recv()
                push(d, t, 0)

        @pl.when(within(t - 4))
        def _():
            for d in (0, 1):
                forward(d, t - 4, 2).wait_recv()

            @pl.when(t >= 6)
            def _():
                sums_sent(t - 6)

            multiply_late(t - 4)

        @pl.when(t == 3)
        def _():
            pltpu.make_async_copy(up, abuf.at[0, :, k], own_l).wait()
            link(up, abuf.at[0, :, 1 - k], own_s, own_r, other).wait_recv()
            send_norms()
            nbuf[0] = nsend[0]

        @pl.when(within(t - 3))
        def _():
            split_early(t - 3)
            multiply_early(t - 3, 2)

        @pl.when(within(t - 5))
        def _():
            add_relays(t - 5)

        @pl.when(t < 3)
        def _():
            basis_block(3 * t + 1)

        @pl.when(within(t - 3))
        def _():
            multiply_early(t - 3, 1)

        @pl.when(within(t - 3))
        def _():
            multiply_early(t - 3, 3)

        @pl.when(within(t - 1))
        def _():
            for d in (0, 1):
                forward(d, t - 1, 0).wait_recv()
                push(d, t - 1, 1)

        @pl.when(t < 2)
        def _():
            basis_block(3 * t + 2)

        @pl.when(within(t - 3))
        def _():
            multiply_early(t - 3, 0)

        @pl.when(within(t - 2))
        def _():
            for d in (0, 1):
                forward(d, t - 2, 1).wait_recv()
                push(d, t - 2, 2)

        @pl.when(t + 4 < nm)
        def _():
            @pl.when(t + 4 >= 4)
            def _():
                for copy in own_copies(t):
                    copy.wait_send()

            for copy in own_copies(t + 4):
                copy.start()

        @pl.when(t == 7)
        def _():
            all_norms.wait_recv()
            total = nbuf[0]
            for slot in range(1, 2 * NY):
                total = total + nbuf[slot]
            sums = jnp.sum(total, axis=0, keepdims=True)
            kept = ssbuf[0, 1, 0:1, :] == 2.0 * child_poles
            scale[...] = jnp.broadcast_to(
                jnp.where(kept, 1.0 / jnp.sqrt(sums), 1.0), (8, nc)
            )

        @pl.when(within(t - 7))
        def _():
            finish(t - 7)

    wbuf[0] = jnp.sum(sq[...], axis=0, keepdims=True)
    for dlt in range(1, n_row):
        link(wbuf.at[0], wbuf.at[n_row - dlt], ws, wr, at_row(dlt)).start()
    all_weights = link(wbuf.at[1:n_row], wbuf.at[1:n_row], ws, wr, other)

    all_poles.wait_send()
    all_shifts.wait_send()
    link(up, abuf.at[0, :, k], own_s, own_r, other).wait_send()
    all_norms.wait_send()

    for m in range(nm - 4, nm):
        for copy in own_copies(m):
            copy.wait_send()
    for m in range(nm - 2, nm):
        for d in (0, 1):
            for stage in (0, 1, 2):
                forward(d, m, stage).wait_send()
        sums_sent(m)
        added_sent(m)

    weight_sum = wbuf[0]
    all_weights.wait_recv()
    for dlt in range(1, n_row):
        weight_sum = weight_sum + wbuf[dlt]
    rows_all = 2 * n_row * nm * half
    slab[...] = weight_sum * (1.0 / rows_all)
    all_weights.wait_send()


def local(n_row, upper_panel, lower_panel, pole_values, coupling, kept_mask, shifts, source):
    rows, kb = upper_panel.shape
    nc = shifts.shape[0]
    nm = CHUNKS
    half = rows // nm
    m2 = 2 * half
    child_poles = NZ * NY * kb
    kpart = NZ * kb
    f32 = jnp.float32
    dma = pltpu.SemaphoreType.DMA
    vmem = pl.BlockSpec(memory_space=pltpu.VMEM)
    hbm = pl.BlockSpec(memory_space=pltpu.HBM)
    out, slab = pl.pallas_call(
        functools.partial(kernel, n_row, child_poles),
        out_shape=(
            jax.ShapeDtypeStruct((2, nm, half, nc), f32),
            jax.ShapeDtypeStruct((1, nc), f32),
        ),
        in_specs=[hbm] * 7,
        out_specs=(vmem, vmem),
        scratch_shapes=[
            pltpu.VMEM((NZ, nm, 2, half, kb), f32),
            pltpu.VMEM((2 * m2, kpart - kb), jnp.bfloat16),
            pltpu.VMEM((2 * m2, kb), jnp.bfloat16),
            pltpu.VMEM((NY, kpart, nc), jnp.bfloat16),
            pltpu.VMEM((NY, kpart, nc), jnp.bfloat16),
            pltpu.VMEM((NY, nm, 2, half, nc), f32),
            pltpu.VMEM((2, nm, half, nc), f32),
            pltpu.VMEM((nm, 5, half, nc), f32),
            pltpu.VMEM((NZ, 8, kb), f32),
            pltpu.VMEM((NY, 2, 8, nc), f32),
            pltpu.VMEM((NY, 8, nc), f32),
            pltpu.VMEM((2 * NY, 8, nc), f32),
            pltpu.VMEM((kb, 128), f32),
            pltpu.VMEM((kb, 128), f32),
            pltpu.VMEM((8, nc), f32),
            pltpu.VMEM((8, nc), f32),
            pltpu.VMEM((n_row, 1, nc), f32),
            pltpu.VMEM((2, kb), f32),
            pltpu.VMEM((2, kb), f32),
            pltpu.VMEM((2, kb), jnp.int32),
            pltpu.VMEM((1, nc), f32),
            pltpu.VMEM((1, nc), jnp.int32),
            dma, dma, dma,
            dma((2, 4, 2)), dma((2, nm)),
            dma((2, 2, 3)), dma((2, nm, 3)),
            dma, dma, dma, dma, dma, dma,
            dma((2, 2)), dma((2, nm)),
            dma((2, 2, 2)), dma((nm,)),
            dma((2,)), dma, dma, dma((5,)),
        ],
        compiler_params=pltpu.CompilerParams(
            collective_id=0, has_side_effects=True, vmem_limit_bytes=50 * 1024 * 1024
        ),
    )(
        *(
            pltpu.with_memory_space_constraint(given, pltpu.HBM)
            for given in (
                upper_panel.reshape(nm, half, kb),
                lower_panel.reshape(nm, half, kb),
                pole_values,
                coupling,
                kept_mask,
                shifts.reshape(1, nc),
                source.reshape(1, nc),
            )
        )
    )
    return out.reshape(2, rows, nc), slab.reshape(nc)


def solution(mesh):
    in_specs = (
        P("row", "col"),
        P("row", "col"),
        P(None, "col"),
        P(None, "col"),
        P(None, "col"),
        P("col"),
        P("col"),
    )
    out_specs = (P(None, "row", "col"), P("col"))
    body = functools.partial(local, mesh.shape["row"])
    return jax.shard_map(body, mesh=mesh, in_specs=in_specs, out_specs=out_specs, check_vma=False)
```

```python
import functools

import jax
import jax.numpy as jnp
from jax import lax
from jax.experimental import pallas as pl
from jax.experimental.pallas import tpu as pltpu
from jax.sharding import PartitionSpec as P

NZ = 8
NY = 4
CHUNKS = 8
LEAD = 5
MESH = pl.DeviceIdType.MESH


def link(src, dst, ssem, rsem, dev):
    return pltpu.make_async_remote_copy(
        src_ref=src, dst_ref=dst, send_sem=ssem, recv_sem=rsem, device_id=dev, device_id_type=MESH
    )


def kernel(
    n_row, child_poles,
    up, lo, poles_in, coup_in, mask_in, shifts_in, source_in,
    out, slab,
    abuf, ahl, atail, bh, bl, pbuf, rbuf, fbuf,
    pwbuf, ssbuf, nsend, nbuf, pcol, wcol, scale, sq, wbuf,
    poles, coup, mask, shifts, source,
    own_l, own_s, own_r, s1, a1, sf, af, pws, pwr, sss, ssr, ns, nr,
    rls, rlr, fs, fr, xs, ws, wr, isem,
):
    r = lax.axis_index("row")
    c = lax.axis_index("col")
    k = lax.rem(r, 2)
    r0 = r - k
    y = lax.div(c, NZ)
    z = lax.rem(c, NZ)
    nm = CHUNKS
    half = up.shape[1]
    kb = up.shape[2]
    m2 = 2 * half
    nc = shifts.shape[1]
    fetches = [
        pltpu.make_async_copy(given, held, isem.at[n])
        for n, (given, held) in enumerate(
            zip(
                (poles_in, coup_in, mask_in, shifts_in, source_in),
                (poles, coup, mask, shifts, source),
            )
        )
    ]
    for fetch in fetches:
        fetch.start()

    def at_z(delta, core):
        return (r0 + core, y * NZ + lax.rem(z + delta + NZ, NZ))

    def at_y(delta, core):
        return (r0 + core, lax.rem(y + delta + NY, NY) * NZ + z)

    def at_row(delta):
        return (lax.rem(r + delta, n_row), c)

    other = (r0 + 1 - k, c)

    barrier = pltpu.get_barrier_semaphore()
    peers = [at_z(d, k) for d in range(1, NZ)] + [at_z(1, 1 - k), at_z(NZ - 1, 1 - k)]
    peers += [at_y(d, q) for d in range(1, NY) for q in (0, 1)]
    peers += [at_row(d) for d in range(1, n_row)]
    for dev in peers:
        pl.semaphore_signal(barrier, inc=1, device_id=dev, device_id_type=MESH)

    for fetch in fetches:
        fetch.wait()
    pw_rows = lax.broadcasted_iota(jnp.int32, (8, kb), 0)
    pole_row = jnp.broadcast_to(poles[pl.ds(k, 1), :], (8, kb))
    weight_row = jnp.broadcast_to(
        coup[pl.ds(k, 1), :] * mask[pl.ds(k, 1), :].astype(jnp.float32), (8, kb)
    )
    pwbuf[0] = jnp.where(pw_rows == 0, pole_row, weight_row)
    ssbuf[0, 0] = jnp.broadcast_to(shifts[...], (8, nc))
    ssbuf[0, 1] = jnp.broadcast_to(source[...].astype(jnp.float32), (8, nc))
    nsend[...] = jnp.zeros_like(nsend)
    sq[...] = jnp.zeros_like(sq)

    pl.semaphore_wait(barrier, len(peers))

    panels = (up, lo)

    def own_copies(m):
        return [
            link(
                panels[child].at[m], abuf.at[NZ - 1 if step == 1 else 1, m, k],
                s1.at[d, m, child], a1.at[d, m], at_z(step, child),
            )
            for d, step in ((0, 1), (1, NZ - 1))
            for child in (0, 1)
        ]

    def first_wait(d, m):
        dst = abuf.at[NZ - 1 if d == 0 else 1, m]
        return link(dst, dst, s1.at[d, 0, 0], a1.at[d, m], other)

    def forward(d, m, stage):
        step = 1 if d == 0 else NZ - 1
        src_rel = NZ - 1 - stage if d == 0 else 1 + stage
        dst_rel = src_rel - 1 if d == 0 else src_rel + 1
        if stage < 2:
            src, dst = abuf.at[src_rel, m], abuf.at[dst_rel, m]
        else:
            src, dst = abuf.at[src_rel, m, d], abuf.at[dst_rel, m, d]
        return link(src, dst, sf.at[d, lax.rem(m, 2), stage], af.at[d, m, stage], at_z(step, k))

    def push(d, m, stage):
        @pl.when(m >= 2)
        def _():
            forward(d, m - 2, stage).wait_send()

        forward(d, m, stage).start()

    for dlt in range(1, NZ):
        link(pwbuf.at[0], pwbuf.at[NZ - dlt], pws, pwr, at_z(dlt, k)).start()
    for dlt in range(1, NY):
        link(ssbuf.at[0], ssbuf.at[NY - dlt], sss, ssr, at_y(dlt, k)).start()
    for m in range(LEAD):
        for copy in own_copies(m):
            copy.start()
    for child in (0, 1):
        local = pltpu.make_async_copy(panels[child], abuf.at[0, :, k], own_l)
        across = link(panels[child], abuf.at[0, :, k], own_s, own_r, other)

        @pl.when(k == child)
        def _():
            local.start()

        @pl.when(k != child)
        def _():
            across.start()

    all_shifts = link(ssbuf.at[1:NY], ssbuf.at[1:NY], sss, ssr, other)
    all_poles = link(pwbuf.at[1:NZ], pwbuf.at[1:NZ], pws, pwr, other)
    all_shifts.wait_recv()
    block_rows = min(64, kb)

    def basis_block(pos):
        rel = pos + lax.div(pos, 4) - 4 * lax.div(pos, NZ - 1)
        pw = pwbuf[rel]
        pcol[...] = jnp.broadcast_to(pw[0:1, :], (128, kb)).T
        wcol[...] = jnp.broadcast_to(pw[1:2, :], (128, kb)).T
        first = k * child_poles + (y * NZ + lax.rem(z + rel, NZ)) * kb

        tall = (block_rows // 8, 8, 128)
        ids = (
            lax.broadcasted_iota(jnp.int32, tall, 0) * 8 + lax.broadcasted_iota(jnp.int32, tall, 1)
        ).astype(jnp.float32)

        @pl.loop(0, NY * (nc // 128))
        def _(tile):
            dest = lax.div(tile, nc // 128)
            lane = pl.multiple_of(lax.rem(tile, nc // 128) * 128, 128)
            shift = ssbuf[dest, 0, :, pl.ds(lane, 128)]
            named = ssbuf[dest, 1, :, pl.ds(lane, 128)]
            kept = named == 2.0 * child_poles
            total = nsend[dest, :, pl.ds(lane, 128)]
            for rb in range(kb // block_rows):
                rows = pl.ds(rb * block_rows, block_rows)
                shape = (block_rows // 8, 8, 128)
                pole = pcol[rows, :].reshape(shape)
                weight = wcol[rows, :].reshape(shape)
                cauchy = weight / (pole - shift[None])
                total = total + jnp.sum(cauchy * cauchy, axis=0)
                at_row_here = named - (first + rb * block_rows).astype(jnp.float32)
                hot = jnp.where(ids == at_row_here[None], 1.0, 0.0)
                value = jnp.where(kept[None], cauchy, hot).reshape(block_rows, 128)
                high = value.astype(jnp.bfloat16)
                low = (value - high.astype(jnp.float32)).astype(jnp.bfloat16)
                at = pl.ds(pl.multiple_of(pos * kb + rb * block_rows, block_rows), block_rows)
                bh[dest, at, pl.ds(lane, 128)] = high
                bl[dest, at, pl.ds(lane, 128)] = low
            nsend[dest, :, pl.ds(lane, 128)] = total

    def send_norms():
        for dlt in range(NY):
            for flip in (0, 1):
                slot = 2 * ((NY - dlt) % NY) + flip
                if slot > 0:
                    core = 1 - k if flip else k
                    link(nsend.at[dlt], nbuf.at[slot], ns, nr, at_y(dlt, core)).start()

    all_norms = link(nbuf.at[1 : 2 * NY], nbuf.at[1 : 2 * NY], ns, nr, other)

    def relay(m, d):
        step = 1 if d == 0 else NY - 1
        return link(
            pbuf.at[2, m, d], rbuf.at[d, m], rls.at[d, lax.rem(m, 2)], rlr.at[d, m], at_y(step, k)
        )

    def final(m, d, o):
        step = 1 if d == 0 else NY - 1
        return link(
            pbuf.at[step, m, o], fbuf.at[m, 2 * k + d], fs.at[d, lax.rem(m, 2), o], fr.at[m],
            at_y(step, o),
        )

    def cross(m):
        return link(pbuf.at[0, m, 1 - k], fbuf.at[m, 4], xs.at[lax.rem(m, 2)], fr.at[m], other)

    def split(rel, m):
        a = abuf[rel, m].reshape(m2, kb)
        high = a.astype(jnp.bfloat16)
        return high, (a - high.astype(jnp.float32)).astype(jnp.bfloat16)

    def split_early(m):
        for pos in range(NZ - 1):
            high, low = split(pos + pos // 4, m)
            ahl[0:m2, pos * kb : (pos + 1) * kb] = high
            ahl[m2 : 2 * m2, pos * kb : (pos + 1) * kb] = low

    early = (NZ - 1) * kb

    def product(a, dest, first, size):
        rows = slice(first, first + size)
        both = jnp.dot(a[...], bh[dest, rows, :], preferred_element_type=jnp.float32)
        rest = jnp.dot(a[0:m2, :], bl[dest, rows, :], preferred_element_type=jnp.float32)
        return (both[0:m2] + (both[m2:] + rest)).reshape(2, half, nc)

    def multiply_early(m, dest):
        pbuf[dest, m] = product(ahl, dest, 0, early)

    def multiply_late(m):
        atail[0:m2, :], atail[m2 : 2 * m2, :] = split(4, m)
        for dest in (2, 1, 3, 0):
            pbuf[dest, m] = pbuf[dest, m] + product(atail, dest, early, kb)
            if dest == 2:
                relay(m, 0).start()
                relay(m, 1).start()
            elif dest == 1:
                final(m, 0, 1).start()
            elif dest == 3:
                final(m, 1, 0).start()
            else:
                cross(m).start()

    def sums_sent(m):
        for d in (0, 1):
            relay(m, d).wait_send()
            final(m, d, 1 - d).wait_send()
        cross(m).wait_send()

    def added_sent(m):
        for d in (0, 1):
            final(m, d, d).wait_send()

    def add_relays(m):
        @pl.when(m >= 2)
        def _():
            added_sent(m - 2)

        relay(m, 0).wait_recv()
        pbuf[1, m, 0] = pbuf[1, m, 0] + rbuf[0, m]
        final(m, 0, 0).start()
        relay(m, 1).wait_recv()
        pbuf[3, m, 1] = pbuf[3, m, 1] + rbuf[1, m]
        final(m, 1, 1).start()

    def finish(m):
        link(fbuf.at[m], fbuf.at[m], xs.at[0], fr.at[m], other).wait_recv()
        factor = scale[0:1, :]
        mine = (pbuf[0, m, k] + (fbuf[m, 2 * k] + fbuf[m, 2 * k + 1])) * factor
        theirs = (fbuf[m, 4] + (fbuf[m, 2 - 2 * k] + fbuf[m, 3 - 2 * k])) * factor
        out[k, m] = mine
        out[1 - k, m] = theirs
        squares = (mine * mine + theirs * theirs).reshape(half // 8, 8, nc)
        sq[...] = sq[...] + jnp.sum(squares, axis=0)

    def within(m):
        return jnp.logical_and(m >= 0, m < nm)

    @pl.loop(0, nm + 7)
    def _(t):
        @pl.when(t < 3)
        def _():
            basis_block(3 * t)

        @pl.when(t == 0)
        def _():
            all_poles.wait_recv()

        @pl.when(within(t))
        def _():
            for d in (0, 1):
                first_wait(d, t).wait_recv()
                push(d, t, 0)

        @pl.when(within(t - 4))
        def _():
            for d in (0, 1):
                forward(d, t - 4, 2).wait_recv()

            @pl.when(t >= 6)
            def _():
                sums_sent(t - 6)

            multiply_late(t - 4)

        @pl.when(t == 3)
        def _():
            pltpu.make_async_copy(up, abuf.at[0, :, k], own_l).wait()
            link(up, abuf.at[0, :, 1 - k], own_s, own_r, other).wait_recv()
            send_norms()
            nbuf[0] = nsend[0]

        @pl.when(within(t - 3))
        def _():
            split_early(t - 3)
            multiply_early(t - 3, 2)

        @pl.when(within(t - 5))
        def _():
            add_relays(t - 5)

        @pl.when(t < 3)
        def _():
            basis_block(3 * t + 1)

        @pl.when(within(t - 3))
        def _():
            multiply_early(t - 3, 1)

        @pl.when(within(t - 3))
        def _():
            multiply_early(t - 3, 3)

        @pl.when(within(t - 1))
        def _():
            for d in (0, 1):
                forward(d, t - 1, 0).wait_recv()
                push(d, t - 1, 1)

        @pl.when(t < 2)
        def _():
            basis_block(3 * t + 2)

        @pl.when(within(t - 3))
        def _():
            multiply_early(t - 3, 0)

        @pl.when(within(t - 2))
        def _():
            for d in (0, 1):
                forward(d, t - 2, 1).wait_recv()
                push(d, t - 2, 2)

        @pl.when(t + 5 < nm)
        def _():
            for copy in own_copies(t + 5):
                copy.start()

        @pl.when(t == 7)
        def _():
            all_norms.wait_recv()
            total = nbuf[0]
            for slot in range(1, 2 * NY):
                total = total + nbuf[slot]
            sums = jnp.sum(total, axis=0, keepdims=True)
            kept = ssbuf[0, 1, 0:1, :] == 2.0 * child_poles
            scale[...] = jnp.broadcast_to(
                jnp.where(kept, 1.0 / jnp.sqrt(sums), 1.0), (8, nc)
            )

        @pl.when(within(t - 7))
        def _():
            finish(t - 7)

    wbuf[0] = jnp.sum(sq[...], axis=0, keepdims=True)
    for dlt in range(1, n_row):
        link(wbuf.at[0], wbuf.at[n_row - dlt], ws, wr, at_row(dlt)).start()
    all_weights = link(wbuf.at[1:n_row], wbuf.at[1:n_row], ws, wr, other)

    all_poles.wait_send()
    all_shifts.wait_send()
    link(up, abuf.at[0, :, k], own_s, own_r, other).wait_send()
    all_norms.wait_send()

    for m in range(nm):
        for copy in own_copies(m):
            copy.wait_send()
    for m in range(nm - 2, nm):
        for d in (0, 1):
            for stage in (0, 1, 2):
                forward(d, m, stage).wait_send()
        sums_sent(m)
        added_sent(m)

    weight_sum = wbuf[0]
    all_weights.wait_recv()
    for dlt in range(1, n_row):
        weight_sum = weight_sum + wbuf[dlt]
    rows_all = 2 * n_row * nm * half
    slab[...] = weight_sum * (1.0 / rows_all)
    all_weights.wait_send()


def local(n_row, upper_panel, lower_panel, pole_values, coupling, kept_mask, shifts, source):
    rows, kb = upper_panel.shape
    nc = shifts.shape[0]
    nm = CHUNKS
    half = rows // nm
    m2 = 2 * half
    child_poles = NZ * NY * kb
    kpart = NZ * kb
    f32 = jnp.float32
    dma = pltpu.SemaphoreType.DMA
    vmem = pl.BlockSpec(memory_space=pltpu.VMEM)
    hbm = pl.BlockSpec(memory_space=pltpu.HBM)
    out, slab = pl.pallas_call(
        functools.partial(kernel, n_row, child_poles),
        out_shape=(
            jax.ShapeDtypeStruct((2, nm, half, nc), f32),
            jax.ShapeDtypeStruct((1, nc), f32),
        ),
        in_specs=[hbm] * 7,
        out_specs=(vmem, vmem),
        scratch_shapes=[
            pltpu.VMEM((NZ, nm, 2, half, kb), f32),
            pltpu.VMEM((2 * m2, kpart - kb), jnp.bfloat16),
            pltpu.VMEM((2 * m2, kb), jnp.bfloat16),
            pltpu.VMEM((NY, kpart, nc), jnp.bfloat16),
            pltpu.VMEM((NY, kpart, nc), jnp.bfloat16),
            pltpu.VMEM((NY, nm, 2, half, nc), f32),
            pltpu.VMEM((2, nm, half, nc), f32),
            pltpu.VMEM((nm, 5, half, nc), f32),
            pltpu.VMEM((NZ, 8, kb), f32),
            pltpu.VMEM((NY, 2, 8, nc), f32),
            pltpu.VMEM((NY, 8, nc), f32),
            pltpu.VMEM((2 * NY, 8, nc), f32),
            pltpu.VMEM((kb, 128), f32),
            pltpu.VMEM((kb, 128), f32),
            pltpu.VMEM((8, nc), f32),
            pltpu.VMEM((8, nc), f32),
            pltpu.VMEM((n_row, 1, nc), f32),
            pltpu.VMEM((2, kb), f32),
            pltpu.VMEM((2, kb), f32),
            pltpu.VMEM((2, kb), jnp.int32),
            pltpu.VMEM((1, nc), f32),
            pltpu.VMEM((1, nc), jnp.int32),
            dma, dma, dma,
            dma((2, nm, 2)), dma((2, nm)),
            dma((2, 2, 3)), dma((2, nm, 3)),
            dma, dma, dma, dma, dma, dma,
            dma((2, 2)), dma((2, nm)),
            dma((2, 2, 2)), dma((nm,)),
            dma((2,)), dma, dma, dma((5,)),
        ],
        compiler_params=pltpu.CompilerParams(
            collective_id=0, has_side_effects=True, vmem_limit_bytes=50 * 1024 * 1024
        ),
    )(
        *(
            pltpu.with_memory_space_constraint(given, pltpu.HBM)
            for given in (
                upper_panel.reshape(nm, half, kb),
                lower_panel.reshape(nm, half, kb),
                pole_values,
                coupling,
                kept_mask,
                shifts.reshape(1, nc),
                source.reshape(1, nc),
            )
        )
    )
    return out.reshape(2, rows, nc), slab.reshape(nc)


def solution(mesh):
    in_specs = (
        P("row", "col"),
        P("row", "col"),
        P(None, "col"),
        P(None, "col"),
        P(None, "col"),
        P("col"),
        P("col"),
    )
    out_specs = (P(None, "row", "col"), P("col"))
    body = functools.partial(local, mesh.shape["row"])
    return jax.shard_map(body, mesh=mesh, in_specs=in_specs, out_specs=out_specs, check_vma=False)
```
